32 devices in a mesh: dp: 4 (over y, x), expert: 8 (over z, core).
Axes of the slice: x: 2, y: 2, z: 4, core: 2. Of those that a mesh axis runs over, the one named last changes fastest.
Arguments:
- tokens: bfloat16 [16, 1024, 2048], P('dp', 'expert'), may hold values from -6 to 6
- cotangent: bfloat16 [16, 1024, 2048], P('dp', 'expert'), may hold values from -6 to 6
- lengths: int32 [16], P('dp'), may hold values from 256 to 1024, as said below
- order: int32 [4, 4], P('dp'), may hold values from 0 to 3, each once within a row
- routes: int32 [16, 1024, 8], P('dp', 'expert'), may hold values from 0 to 15, all different within a row
- attn_norm: bfloat16 [2048], P(('dp', 'expert')), may hold values from 0.099609375 to 1.8984375
- query_weight: bfloat16 [2048, 2048], P(('dp', 'expert')), may hold values from -0.125 to 0.125
- key_weight: bfloat16 [2048, 2048], P(('dp', 'expert')), may hold values from -0.125 to 0.125
- value_weight: bfloat16 [2048, 2048], P(('dp', 'expert')), may hold values from -0.125 to 0.125
- q_norm: bfloat16 [128], replicated, may hold values from 0.099609375 to 1.8984375
- k_norm: bfloat16 [128], replicated, may hold values from 0.099609375 to 1.8984375
- output_weight: bfloat16 [2048, 2048], P(('dp', 'expert')), may hold values from -2 to 2
- ffn_norm: bfloat16 [2048], P(('dp', 'expert')), may hold values from 0.099609375 to 1.8984375
- w_router: bfloat16 [2048, 16], P(('dp', 'expert')), may hold values from -0.0625 to 0.0625
- w_gate: bfloat16 [16, 2048, 1024], P('expert', 'dp'), may hold values from -0.125 to 0.125
- w_up: bfloat16 [16, 2048, 1024], P('expert', 'dp'), may hold values from -0.125 to 0.125
- w_down: bfloat16 [16, 1024, 2048], P('expert', 'dp'), may hold values from -0.375 to 0.375
Outputs:
- layer_out: bfloat16 [16, 1024, 2048], P('dp', 'expert')
- grad_tokens: float32 [16, 1024, 2048], P('dp', 'expert')
- grad_attn_norm: float32 [2048], P(('dp', 'expert'))
- grad_query: float32 [2048, 2048], P(('dp', 'expert'))
- grad_key: float32 [2048, 2048], P(('dp', 'expert'))
- grad_value: float32 [2048, 2048], P(('dp', 'expert'))
- grad_q_norm: float32 [128], replicated
- grad_k_norm: float32 [128], replicated
- grad_out: float32 [2048, 2048], P(('dp', 'expert'))
- grad_ffn_norm: float32 [2048], P(('dp', 'expert'))
- grad_router: float32 [2048, 16], P(('dp', 'expert'))
- grad_gate: float32 [16, 2048, 1024], P('expert', 'dp')
- grad_up: float32 [16, 2048, 1024], P('expert', 'dp')
- grad_down: float32 [16, 1024, 2048], P('expert', 'dp')
The draws below stay inside these ranges and needn't reach their ends.
Inputs may be any that keep to these rules, and one draw needn't show every extreme that they name: Sequence s has lengths[s] live positions, the first ones; the rest is padding. Row g deals the 4 sequences of data group g, by local index: micro-batch m takes entries m * 2 to (m + 1) * 2 - 1 in that order. `routes`: each token names 8 different experts.
All inputs are finite; a program needn't handle non-finite values.
Results may differ from the reference program's by a relative error of at most 0.019.
Values may be sent and summed in bfloat16 or wider, within the bound.
No kernel may reach another device: no remote copies, remote signals or barrier semaphores. Data moves between devices by JAX's collectives and lax.ppermute only.
A program may use at most 448 MiB of HBM per device.

```python
import jax
import jax.numpy as jnp
from jax import lax

D = 2048
HEAD_COUNT = 16
HEAD_WIDTH = 128
FF = 1024
TOP = 8
SEQUENCE_LENGTH = 1024
SEQ_MB = 2
MICRO = 2
EXPERTS = 16
SEQ_DP = 4
SEQS = 16
GROUPS = 4
CAP = 128
N_DP = 4
N_EXPERT = 8


def draw_lengths(key, part):
    values = jax.random.randint(key, (SEQS,), SEQUENCE_LENGTH // 4, SEQUENCE_LENGTH + 1, dtype=jnp.int32)
    return values.at[0].set(SEQUENCE_LENGTH).at[1].set(SEQUENCE_LENGTH // 4)


def shard_levels(stream_key, extent, pieces, low, high):
    loudness = 1.0
    for dim, shards_of in pieces:
        steps = jax.random.uniform(jax.random.fold_in(jax.random.fold_in(stream_key, 6), dim), (shards_of,), jnp.float32, low / len(pieces), high / len(pieces))
        loudness = loudness * jnp.repeat(jnp.exp(steps), extent[dim] // shards_of).reshape((-1,) + (1,) * (len(extent) - 1 - dim))
    return loudness


def different_ones(rng, rows, amount, top, lift):
    order = jax.random.permutation(jax.random.fold_in(rng, 1), amount)
    favour = order
    for power in range(3):
        favour = favour * favour // amount
    favour = favour * lift // amount
    tickets = jax.random.randint(jax.random.fold_in(rng, 2), (rows, amount), 0, 4096) + favour
    fixed_rows = jax.random.permutation(jax.random.fold_in(rng, 3), rows)[jnp.arange(amount) % rows]
    tickets = jnp.where(jnp.arange(rows)[:, None] == fixed_rows[None, :], 1 << 14, tickets)
    score = tickets * amount + jnp.arange(amount)
    return lax.top_k(score.astype(jnp.int32), top)[1].astype(jnp.int32)


def bell_draw(stream_key, extent, scale, most, shards=(), kind=jnp.bfloat16):
    entries = scale * jax.random.normal(stream_key, extent, jnp.float32)
    if shards:
        entries = entries * shard_levels(stream_key, extent, shards, -0.22, 0.18)
    return jnp.clip(entries, -most, most).astype(kind)


def setup_inputs(seed: int = 0) -> dict:
    seeds = jax.random.split(jax.random.key(seed), 18)
    return {
        "tokens": bell_draw(seeds[0], (SEQS, SEQUENCE_LENGTH, D), 1.0, 6.0, ((0, 4), (1, 8))),
        "cotangent": bell_draw(seeds[1], (SEQS, SEQUENCE_LENGTH, D), 1.0, 6.0, ((0, 4), (1, 8))),
        "lengths": draw_lengths(jax.random.fold_in(seeds[17], 71), 0),
        "order": jax.vmap(lambda own: jax.random.permutation(own, SEQ_DP))(jax.random.split(seeds[3], GROUPS)).reshape((GROUPS, SEQ_DP)).astype(jnp.int32),
        "routes": different_ones(seeds[4], SEQS * SEQUENCE_LENGTH, EXPERTS, TOP, 4096).reshape((SEQS, SEQUENCE_LENGTH, TOP)),
        "attn_norm": jnp.clip(1.0 + 0.18 * jax.random.normal(seeds[5], (D,), jnp.float32), 0.099609375, 1.8984375).astype(jnp.bfloat16),
        "query_weight": bell_draw(seeds[6], (D, D), D ** -0.5, 0.125, ((0, 32),)),
        "key_weight": bell_draw(seeds[7], (D, D), D ** -0.5, 0.125, ((0, 32),)),
        "value_weight": bell_draw(seeds[8], (D, D), D ** -0.5, 0.125, ((0, 32),)),
        "q_norm": jnp.clip(1.0 + 0.18 * jax.random.normal(seeds[9], (HEAD_WIDTH,), jnp.float32), 0.099609375, 1.8984375).astype(jnp.bfloat16),
        "k_norm": jnp.clip(1.0 + 0.18 * jax.random.normal(seeds[10], (HEAD_WIDTH,), jnp.float32), 0.099609375, 1.8984375).astype(jnp.bfloat16),
        "output_weight": bell_draw(seeds[11], (D, D), (max(D // 256, 1)) ** -0.5, 2.0, ((0, 32),)),
        "ffn_norm": jnp.clip(1.0 + 0.18 * jax.random.normal(seeds[12], (D,), jnp.float32), 0.099609375, 1.8984375).astype(jnp.bfloat16),
        "w_router": bell_draw(seeds[13], (D, EXPERTS), (4 * D) ** -0.5, 0.0625, ((0, 32),)),
        "w_gate": bell_draw(seeds[14], (EXPERTS, D, FF), D ** -0.5, 0.125, ((0, 8), (1, 4))),
        "w_up": bell_draw(seeds[15], (EXPERTS, D, FF), D ** -0.5, 0.125, ((0, 8), (1, 4))),
        "w_down": bell_draw(seeds[16], (EXPERTS, FF, D), (FF // 4) ** -0.5, 0.375, ((0, 8), (1, 4))),
    }


@jax.custom_vjp
def low(v):
    return lax.optimization_barrier(v.astype(jnp.bfloat16)).astype(jnp.float32)

@jax.custom_vjp
def low_back(v):
    return v

def low_keep(v):
    return (low(v), None)

def low_pass(kept, grad):
    return (grad,)

def back_keep(v):
    return (v, None)

def back_low(kept, grad):
    return (low(grad),)
low.defvjp(low_keep, low_pass)
low_back.defvjp(back_keep, back_low)
PRECISE_MODE = lax.Precision.HIGHEST
EPS = 1e-06
NEG = -1e+30
THETA = 10000.0

def rounded_pair(values):
    return low_back(low(values))

def norm_rows(values, gain):
    return values * lax.rsqrt(lax.optimization_barrier(jnp.mean(values * values, axis=-1, keepdims=True)) + EPS) * gain

def rope_tables(positions):
    half_dim = HEAD_WIDTH // 2
    inverse = THETA ** (-(2.0 * jnp.arange(half_dim, dtype=jnp.float32)) / HEAD_WIDTH)
    angles = positions.astype(jnp.float32)[:, None] * inverse[None, :]
    return (jnp.cos(angles), jnp.sin(angles))

def rotate(values, cosine, sine):
    half_dim = values.shape[-1] // 2
    first = values[..., :half_dim]
    second = values[..., half_dim:]
    return jnp.concatenate([first * cosine - second * sine, second * cosine + first * sine], axis=-1)

def to_device(values):
    shape = values.shape
    seg_len = shape[1] // N_EXPERT
    split = values.reshape((shape[0], N_EXPERT, seg_len) + shape[2:])
    moved = jnp.moveaxis(split, 1, 0)
    return moved.reshape((N_EXPERT, shape[0] * seg_len) + shape[2:])

def from_device(values, sequence_count):
    shape = values.shape
    seg_len = shape[1] // sequence_count
    split = values.reshape((N_EXPERT, sequence_count, seg_len) + shape[2:])
    moved = jnp.moveaxis(split, 0, 1)
    return moved.reshape((sequence_count, N_EXPERT * seg_len) + shape[2:])

def slot_plan(route_rows, live_rows, experts, capacity):
    tok_count = route_rows.shape[0]
    flat_routes = route_rows.reshape(-1).astype(jnp.int32)
    alive = jnp.repeat(live_rows.astype(jnp.int32), TOP)
    hits = (flat_routes[:, None] == jnp.arange(experts, dtype=jnp.int32)[None, :]).astype(jnp.int32) * alive[:, None]
    earlier = (jnp.cumsum(hits, axis=0) - hits).astype(jnp.int32)
    ranking = lax.optimization_barrier(jnp.sum(earlier * hits, axis=1)).astype(jnp.int32)
    keeping = (alive > 0) & (ranking < capacity)
    dest = jnp.where(keeping, flat_routes * capacity + ranking, experts * capacity).astype(jnp.int32)
    owners = jnp.repeat(jnp.arange(tok_count, dtype=jnp.int32), TOP)
    slot_token = jnp.full((experts * capacity,), tok_count, jnp.int32).at[dest].set(owners, mode='drop')
    return (dest.reshape(route_rows.shape), slot_token)

def take_rows(table, indices):
    return jnp.take(table, indices.reshape(-1), axis=0)

def forward(params, input_rows, live, route_dev, dest, slot_token):
    gain_in, query_weight, key_weight, value_weight, gain_q, gain_k, output_weight, gain_ffn, w_router, w_gate, w_up, w_down = params
    sequence_count = input_rows.shape[0]
    cosine, sine = rope_tables(jnp.arange(SEQUENCE_LENGTH, dtype=jnp.int32))
    cosine = cosine[None, :, None, :]
    sine = sine[None, :, None, :]
    normalized_rows = low(norm_rows(input_rows, gain_in))
    query_projected = low_back(jnp.einsum('kgn,nr->kgr', normalized_rows, query_weight, precision=PRECISE_MODE)).reshape(sequence_count, SEQUENCE_LENGTH, HEAD_COUNT, HEAD_WIDTH)
    key_projected = low_back(jnp.einsum('kgn,nr->kgr', normalized_rows, key_weight, precision=PRECISE_MODE)).reshape(sequence_count, SEQUENCE_LENGTH, HEAD_COUNT, HEAD_WIDTH)
    value_projected = rounded_pair(jnp.einsum('kgn,nr->kgr', normalized_rows, value_weight, precision=PRECISE_MODE)).reshape(sequence_count, SEQUENCE_LENGTH, HEAD_COUNT, HEAD_WIDTH)
    q_rot = rounded_pair(rotate(norm_rows(query_projected, gain_q), cosine, sine))
    k_rot = rounded_pair(rotate(norm_rows(key_projected, gain_k), cosine, sine))
    scores = low_back(jnp.einsum('sqhe,skhe->shqk', q_rot, k_rot, precision=PRECISE_MODE) * HEAD_WIDTH ** (-0.5))
    scores = jnp.where(live[:, None, None, :], scores, NEG)
    peak = lax.optimization_barrier(jnp.max(scores, axis=-1, keepdims=True))
    expo = jnp.exp(scores - peak)
    probs = expo / lax.optimization_barrier(jnp.sum(expo, axis=-1, keepdims=True))
    mixed_output = rounded_pair(jnp.einsum('shqk,skhe->sqhe', low(probs), value_projected, precision=PRECISE_MODE)).reshape(sequence_count, SEQUENCE_LENGTH, D)
    hidden_state = input_rows + low_back(jnp.einsum('kgn,nr->kgr', mixed_output, output_weight, precision=PRECISE_MODE))
    routed = low(norm_rows(hidden_state, gain_ffn))
    dev_rows = to_device(routed)
    logits = jnp.einsum('etd,dj->etj', dev_rows, w_router, precision=PRECISE_MODE)
    chosen = jnp.take_along_axis(logits, route_dev, axis=-1)
    chosen_peak = lax.optimization_barrier(jnp.max(chosen, axis=-1, keepdims=True))
    chosen_exp = jnp.exp(chosen - chosen_peak)
    gates = chosen_exp / lax.optimization_barrier(jnp.sum(chosen_exp, axis=-1, keepdims=True))
    padded = jnp.concatenate([dev_rows, jnp.zeros((N_EXPERT, 1, D), jnp.float32)], axis=1)
    sent = low_back(jax.vmap(take_rows)(padded, slot_token)).reshape(N_EXPERT, EXPERTS, CAP, D)
    gate_pre = low_back(jnp.einsum('sjcd,jdf->sjcf', sent, w_gate, precision=PRECISE_MODE))
    up_pre = low_back(jnp.einsum('sjcd,jdf->sjcf', sent, w_up, precision=PRECISE_MODE))
    act = low(gate_pre / (1.0 + jnp.exp(-gate_pre)) * up_pre)
    made = rounded_pair(jnp.einsum('sjcf,jfd->sjcd', act, w_down, precision=PRECISE_MODE)).reshape(N_EXPERT, EXPERTS * CAP, D)
    made = jnp.concatenate([made, jnp.zeros((N_EXPERT, 1, D), jnp.float32)], axis=1)
    picked = jax.vmap(take_rows)(made, dest).reshape(N_EXPERT, -1, TOP, D)
    mixture = lax.optimization_barrier(jnp.sum(gates[..., None] * picked, axis=2))
    return live[..., None].astype(jnp.float32) * (hidden_state + from_device(mixture, sequence_count))

def reference(tokens, cotangent, lengths, order, routes, attn_norm, query_weight, key_weight, value_weight, q_norm, k_norm, output_weight, ffn_norm, w_router, w_gate, w_up, w_down):
    params = tuple((weight.astype(jnp.float32) for weight in (attn_norm, query_weight, key_weight, value_weight, q_norm, k_norm, output_weight, ffn_norm, w_router, w_gate, w_up, w_down)))
    spots = jnp.arange(SEQUENCE_LENGTH, dtype=jnp.int32)

    def micro_step(totals, step_index):
        group = step_index // MICRO
        micro_index = step_index % MICRO
        picks = lax.dynamic_slice_in_dim(order[group], (micro_index * SEQ_MB).astype(jnp.int32), SEQ_MB).astype(jnp.int32)
        seq_rows = (group * SEQ_DP + picks).astype(jnp.int32)
        input_rows = tokens[seq_rows].astype(jnp.float32)
        live = spots[None, :] < lengths[seq_rows][:, None]
        route_dev = to_device(routes[seq_rows]).astype(jnp.int32)
        live_dev = to_device(live)
        dest, slot_token = jax.vmap(lambda route_rows, live_rows: slot_plan(route_rows, live_rows, EXPERTS, CAP))(route_dev, live_dev)
        result, pull = jax.vjp(lambda weights, values: forward(weights, values, live, route_dev, dest, slot_token), params, input_rows)
        grads, back = pull(cotangent[seq_rows].astype(jnp.float32))
        totals = tuple((total + grad for total, grad in zip(totals, grads)))
        return (totals, (seq_rows, result, back))
    zeros = tuple((jnp.zeros_like(weight) for weight in params))
    totals, (seq_rows, results, backs) = lax.scan(micro_step, zeros, jnp.arange(N_DP * MICRO, dtype=jnp.int32))
    flat_rows = seq_rows.reshape(-1)
    layer_out = jnp.zeros((SEQS, SEQUENCE_LENGTH, D), jnp.float32).at[flat_rows].set(results.reshape(-1, SEQUENCE_LENGTH, D)).astype(jnp.bfloat16)
    grad_tokens = jnp.zeros((SEQS, SEQUENCE_LENGTH, D), jnp.float32).at[flat_rows].set(backs.reshape(-1, SEQUENCE_LENGTH, D))
    return (layer_out, grad_tokens, totals[0], totals[1], totals[2], totals[3], totals[4], totals[5], totals[6], totals[7], totals[8], totals[9], totals[10], totals[11])
```

```python
import functools

import jax
import jax.numpy as jnp
from jax import lax
from jax.experimental import pallas as pl
from jax.experimental.pallas import tpu as pltpu
from jax.sharding import PartitionSpec as P

D = 2048
HEAD_COUNT = 16
HEAD_WIDTH = 128
TOP = 8
SEQ_MB = 2
MICRO = 2

EPS = 1e-06
NEG = -1e30
THETA = 10000.0
SCALE = HEAD_WIDTH ** (-0.5)
BF = jnp.bfloat16
F32 = jnp.float32


def dot(a, b):
    return lax.dot_general(a, b, (((1,), (0,)), ((), ())), preferred_element_type=F32)


def dot_nt(a, b):
    return lax.dot_general(a, b, (((1,), (1,)), ((), ())), preferred_element_type=F32)


def dot_tn(a, b):
    return lax.dot_general(a, b, (((0,), (0,)), ((), ())), preferred_element_type=F32)


def norm_factor(values):
    return lax.rsqrt(jnp.mean(values * values, axis=-1, keepdims=True) + EPS)


def norm_back(grad_after, rows, factor, gain):
    scaled = grad_after * gain
    shift = jnp.mean(scaled * rows, axis=-1, keepdims=True)
    return factor * scaled - rows * (factor * factor * factor * shift)


def swap_halves(values):
    return pltpu.roll(values, HEAD_WIDTH // 2, 1)


def head_columns(ref, index, length):
    cols = ref[:, 0, :, index * HEAD_WIDTH : (index + 1) * HEAD_WIDTH]
    return cols.reshape(length, HEAD_WIDTH)


def rotated(rows, gain, cosine, sine):
    factor = norm_factor(rows)
    normed = rows * factor * gain
    return (normed * cosine + swap_halves(normed) * sine).astype(BF), factor


def attend_kernel(
    qkv_ref, cos_ref, sin_ref, gains_ref, keep_ref, mixed_ref, lse_ref, *, heads, tile
):
    blocks, _, seg, _ = qkv_ref.shape
    length = blocks * seg
    cosine = cos_ref[...]
    sine = sin_ref[...]
    keep = keep_ref[0] > 0
    for head in range(heads):
        q_rot, _ = rotated(head_columns(qkv_ref, head, length), gains_ref[0:1], cosine, sine)
        k_rot, _ = rotated(
            head_columns(qkv_ref, heads + head, length), gains_ref[1:2], cosine, sine
        )
        values = head_columns(qkv_ref, 2 * heads + head, length).astype(BF)
        for step in range(length // tile):
            rows = slice(step * tile, (step + 1) * tile)
            scores = jnp.where(keep, dot_nt(q_rot[rows], k_rot) * SCALE, NEG)
            peak = jnp.max(scores, axis=-1, keepdims=True)
            expo = jnp.exp(scores - peak)
            total = jnp.sum(expo, axis=-1, keepdims=True)
            mixed = dot((expo * (1.0 / total)).astype(BF), values)
            first = step * tile // seg
            mixed_ref[
                first : first + tile // seg, 0, :, head * HEAD_WIDTH : (head + 1) * HEAD_WIDTH
            ] = mixed.astype(BF).reshape(tile // seg, seg, HEAD_WIDTH)
            lse_ref[0, head, rows, :] = jnp.broadcast_to(
                peak + jnp.log(total), (tile, HEAD_WIDTH)
            )


def attend_back_kernel(
    qkv_ref,
    grad_ref,
    lse_ref,
    cos_ref,
    sin_ref,
    gains_ref,
    keep_ref,
    out_ref,
    gain_ref,
    dq_ref,
    dk_ref,
    dv_ref,
    *,
    heads,
    tile,
):
    blocks, _, seg, _ = qkv_ref.shape
    length = blocks * seg
    cosine = cos_ref[...]
    sine = sin_ref[...]
    keep = keep_ref[0] > 0
    gain_sums = [jnp.zeros((1, HEAD_WIDTH), F32), jnp.zeros((1, HEAD_WIDTH), F32)]

    def store(index, rows):
        out_ref[:, 0, :, index * HEAD_WIDTH : (index + 1) * HEAD_WIDTH] = rows.astype(BF).reshape(
            blocks, seg, HEAD_WIDTH
        )

    for head in range(heads):
        q_rows = head_columns(qkv_ref, head, length)
        k_rows = head_columns(qkv_ref, heads + head, length)
        q_rot, q_factor = rotated(q_rows, gains_ref[0:1], cosine, sine)
        k_rot, k_factor = rotated(k_rows, gains_ref[1:2], cosine, sine)
        values = head_columns(qkv_ref, 2 * heads + head, length).astype(BF)
        grads = head_columns(grad_ref, head, length)
        for step in range(length // tile):
            rows = slice(step * tile, (step + 1) * tile)
            scores = jnp.where(keep, dot_nt(q_rot[rows], k_rot) * SCALE, NEG)
            probs = jnp.exp(scores - lse_ref[0, head, rows, 0:1])
            grad_probs = dot_nt(grads[rows], values)
            inner = jnp.sum(probs * grad_probs, axis=-1, keepdims=True)
            grad_scores = (probs * (grad_probs - inner)).astype(BF)
            dq_ref[rows, :] = dot(grad_scores, k_rot) * SCALE
            dk = dot_tn(grad_scores, q_rot[rows])
            dv = dot_tn(probs.astype(BF), grads[rows])
            if step == 0:
                dk_ref[...] = dk
                dv_ref[...] = dv
            else:
                dk_ref[...] += dk
                dv_ref[...] += dv
        for which, (acc_ref, factor, source, scale) in enumerate(
            ((dq_ref, q_factor, q_rows, 1.0), (dk_ref, k_factor, k_rows, SCALE))
        ):
            grad = acc_ref[...] * scale
            grad = grad * cosine - swap_halves(grad) * sine
            gain_sums[which] += jnp.sum(grad * source * factor, axis=0, keepdims=True)
            store(
                which * heads + head,
                norm_back(grad, source, factor, gains_ref[which : which + 1]),
            )
        store(2 * heads + head, dv_ref[...])
    gain_ref[0] = jnp.concatenate(gain_sums, axis=0)


def attend(qkv, cosine, sine, gains, keep):
    blocks, seqs, seg, width = qkv.shape
    length = blocks * seg
    heads = width // (3 * HEAD_WIDTH)
    tile = max(length // 4, seg)
    full = lambda shape: pl.BlockSpec(shape, lambda s: (0,) * len(shape))
    return pl.pallas_call(
        functools.partial(attend_kernel, heads=heads, tile=tile),
        grid=(seqs,),
        in_specs=[
            pl.BlockSpec((blocks, 1, seg, width), lambda s: (0, s, 0, 0)),
            full((length, HEAD_WIDTH)),
            full((length, HEAD_WIDTH)),
            full((2, HEAD_WIDTH)),
            pl.BlockSpec((1, 1, length), lambda s: (s, 0, 0)),
        ],
        out_specs=[
            pl.BlockSpec((blocks, 1, seg, heads * HEAD_WIDTH), lambda s: (0, s, 0, 0)),
            pl.BlockSpec((1, heads, length, HEAD_WIDTH), lambda s: (s, 0, 0, 0)),
        ],
        out_shape=[
            jax.ShapeDtypeStruct((blocks, seqs, seg, heads * HEAD_WIDTH), BF),
            jax.ShapeDtypeStruct((seqs, heads, length, HEAD_WIDTH), F32),
        ],
        name="attend",
    )(qkv, cosine, sine, gains, keep)


def attend_back(qkv, grads, lse, cosine, sine, gains, keep):
    blocks, seqs, seg, width = qkv.shape
    length = blocks * seg
    heads = width // (3 * HEAD_WIDTH)
    tile = max(length // 4, seg)
    full = lambda shape: pl.BlockSpec(shape, lambda s: (0,) * len(shape))
    return pl.pallas_call(
        functools.partial(attend_back_kernel, heads=heads, tile=tile),
        grid=(seqs,),
        in_specs=[
            pl.BlockSpec((blocks, 1, seg, width), lambda s: (0, s, 0, 0)),
            pl.BlockSpec((blocks, 1, seg, heads * HEAD_WIDTH), lambda s: (0, s, 0, 0)),
            pl.BlockSpec((1, heads, length, HEAD_WIDTH), lambda s: (s, 0, 0, 0)),
            full((length, HEAD_WIDTH)),
            full((length, HEAD_WIDTH)),
            full((2, HEAD_WIDTH)),
            pl.BlockSpec((1, 1, length), lambda s: (s, 0, 0)),
        ],
        out_specs=[
            pl.BlockSpec((blocks, 1, seg, width), lambda s: (0, s, 0, 0)),
            pl.BlockSpec((1, 2, HEAD_WIDTH), lambda s: (s, 0, 0)),
        ],
        out_shape=[
            jax.ShapeDtypeStruct((blocks, seqs, seg, width), BF),
            jax.ShapeDtypeStruct((seqs, 2, HEAD_WIDTH), F32),
        ],
        scratch_shapes=[pltpu.VMEM((length, HEAD_WIDTH), F32)] * 3,
        name="attend_back",
    )(qkv, grads, lse, cosine, sine, gains, keep)


def hop(value, chips, first, last, move):
    pairs = [(2 * s + k, 2 * (s + move) + k) for s in range(first, last) for k in (0, 1)]
    return lax.ppermute(value, "expert", pairs)


def exchange(value, ways):
    return lax.ppermute(value, "expert", [(e, e ^ 1) for e in range(ways)])


def spread(block, chip, ways):
    chips = ways // 2
    ups, downs = [block], [block]
    for h in range(1, chips):
        ups.append(hop(ups[-1], chips, h - 1, chips - 1, 1))
        downs.append(hop(downs[-1], chips, 1, chips - h + 1, -1))
    own = [block]
    for h in range(1, chips):
        own.append(jnp.where(chip >= h, ups[h], downs[chips - h]))
    other = [exchange(value, ways) for value in own]
    return own + other


def collect(parts, ways):
    chips = ways // 2
    sums = [None] * chips
    order = sorted(range(chips), key=lambda h: -max(h, (chips - h) % chips))
    for h in order:
        sums[h] = parts[h].astype(F32) + exchange(parts[chips + h], ways).astype(F32)
    down = up = None
    for t in range(chips - 1, 0, -1):
        below = sums[t] if down is None else sums[t] + down.astype(F32)
        above = sums[chips - t] if up is None else sums[chips - t] + up.astype(F32)
        down = hop(below.astype(BF), chips, t, chips, -1)
        up = hop(above.astype(BF), chips, 0, chips - t, 1)
    return sums[0] + down.astype(F32) + up.astype(F32)


def take_major(array, index):
    return lax.dynamic_index_in_dim(array, index, 0, keepdims=False)


def body(
    tokens,
    cotangent,
    lengths,
    order,
    routes,
    attn_norm,
    query_weight,
    key_weight,
    value_weight,
    q_norm,
    k_norm,
    output_weight,
    ffn_norm,
    w_router,
    w_gate,
    w_up,
    w_down,
):
    both = ("dp", "expert")
    dps = lax.axis_size("dp")
    ways = lax.axis_size("expert")
    chips = ways // 2
    me = lax.axis_index("expert")
    chip, core = me // 2, me % 2
    seqs, seg, _ = tokens.shape
    length = seg * ways
    blk = SEQ_MB * seg
    own_rows = attn_norm.shape[0]
    experts = w_router.shape[1]
    capacity = blk * TOP // experts
    local = w_gate.shape[0]
    ff = w_gate.shape[2]
    hcols = D // ways
    slots = ways * capacity

    sources = jnp.stack(
        [((chip + chips - h) % chips) * 2 + (core ^ cc) for cc in (0, 1) for h in range(chips)]
    )
    positions = (sources[:, None] * seg + jnp.arange(seg, dtype=jnp.int32)[None, :]).reshape(length)
    inverse = THETA ** (-(2.0 * jnp.arange(HEAD_WIDTH // 2, dtype=F32)) / HEAD_WIDTH)
    angles = positions.astype(F32)[:, None] * inverse[None, :]
    cosine = jnp.concatenate([jnp.cos(angles)] * 2, axis=1)
    sine = jnp.concatenate([-jnp.sin(angles), jnp.sin(angles)], axis=1)
    gains = jnp.stack([q_norm, k_norm]).astype(F32)

    route_cols = routes.astype(BF).reshape(own_rows, -1)
    small = lax.all_gather(
        jnp.concatenate([w_router, attn_norm[:, None], ffn_norm[:, None], route_cols], axis=1),
        both,
        axis=0,
        tiled=True,
    )
    router = small[:, :experts]
    gain_in = small[:, experts].astype(F32)[None, :]
    gain_ffn = small[:, experts + 1].astype(F32)[None, :]
    all_routes = lax.dynamic_index_in_dim(
        small[:, experts + 2 :].reshape(dps, ways, own_rows, -1),
        lax.axis_index("dp"),
        0,
        keepdims=False,
    ).reshape(ways, seqs, seg, TOP)
    all_routes = jnp.take(all_routes, sources, axis=0).transpose(1, 0, 3, 2)

    split = lambda weight: weight.reshape(own_rows, ways, hcols)
    qkv_part = jnp.concatenate(
        [split(query_weight), split(key_weight), split(value_weight)], axis=2
    ).transpose(1, 0, 2)
    qkv_part = lax.all_to_all(qkv_part, "expert", split_axis=0, concat_axis=0, tiled=True)
    w_qkv = lax.all_gather(
        qkv_part.reshape(ways * own_rows, 3 * hcols), "dp", axis=0, tiled=True
    )
    owner_pairs = [(r, (r % dps) * ways + r // dps) for r in range(dps * ways)]
    w_out = lax.all_gather(
        lax.ppermute(output_weight, both, owner_pairs), "dp", axis=0, tiled=True
    )
    gate_full = lax.all_gather(w_gate, "dp", axis=1, tiled=True)
    up_full = lax.all_gather(w_up, "dp", axis=1, tiled=True)
    down_full = lax.all_gather(w_down, "dp", axis=1, tiled=True)

    strict = (
        jnp.arange(blk, dtype=jnp.int32)[:, None] < jnp.arange(blk, dtype=jnp.int32)[None, :]
    ).astype(BF)
    slot_ids = jnp.arange(capacity, dtype=jnp.int32)[None, :, None]
    expert_ids = jnp.arange(experts, dtype=jnp.int32)

    outputs = jnp.zeros(tokens.shape, BF)
    input_grads = jnp.zeros(tokens.shape, F32)
    g_qkv_weight = g_out_weight = g_router = g_ffn_gain = g_head_gains = None
    expert_rows = []

    def add(total, part):
        return part if total is None else total + part

    state = []
    for micro in range(MICRO):
        picks = [order[0, micro * SEQ_MB + i] for i in range(SEQ_MB)]
        rows_of = lambda array: jnp.concatenate([take_major(array, p) for p in picks], axis=0)
        input_rows = rows_of(tokens)
        seq_lens = jnp.stack([lengths[p] for p in picks])
        live_at = positions[None, :] < seq_lens[:, None]
        keep = live_at.astype(F32)[:, None, :]
        live_col = live_at.reshape(SEQ_MB, ways, seg)[:, 0].reshape(blk, 1).astype(F32)

        gathered = spread(input_rows, chip, ways)
        normed = jnp.concatenate(
            [
                (b * norm_factor(b) * gain_in).astype(BF)
                for b in (block.astype(F32) for block in gathered)
            ],
            axis=0,
        )
        qkv = dot(normed, w_qkv).reshape(ways, SEQ_MB, seg, 3 * hcols)
        mixed, lse = attend(qkv, cosine, sine, gains, keep)
        mixed = mixed.reshape(ways * blk, hcols)
        out_parts = dot(mixed, w_out).astype(BF).reshape(ways, blk, D)
        tokens_f32 = input_rows.astype(F32)
        hidden = tokens_f32 + collect([out_parts[b] for b in range(ways)], ways)
        factor_ffn = norm_factor(hidden)
        routed = (hidden * factor_ffn * gain_ffn).astype(BF)

        routed_all = jnp.concatenate(spread(routed, chip, ways), axis=0)
        grad_rows = rows_of(cotangent)
        grad_all = jnp.concatenate(spread(grad_rows, chip, ways), axis=0).reshape(ways, blk, D)
        picked = jnp.stack([take_major(all_routes, p) for p in picks], axis=2)
        picked = picked.reshape(ways, TOP, blk).astype(jnp.int32)
        alive = live_at.reshape(SEQ_MB, ways, seg).transpose(1, 0, 2).reshape(ways, blk)
        logits = lax.dot_general(
            router, routed_all, (((0,), (1,)), ((), ())), preferred_element_type=F32
        ).reshape(experts, ways, blk)
        chosen = jnp.any(picked[None] == expert_ids[:, None, None, None], axis=2)
        masked = jnp.where(chosen, logits, NEG)
        expo = jnp.exp(masked - jnp.max(masked, axis=0, keepdims=True))
        gates = expo / jnp.sum(expo, axis=0, keepdims=True)
        routed_blocks = routed_all.reshape(ways, blk, D)
        backs = []
        mixtures = grads_routed = None
        gate_grads = []
        for j in range(local):
            mine = me * local + j
            hits = jnp.any(picked == mine, axis=1) & alive
            rank = dot(hits.astype(BF), strict).astype(jnp.int32)
            select = ((rank[:, None, :] == slot_ids) & hits[:, None, :]).astype(BF)
            gate = take_major(gates, mine)
            slot_gate = jnp.sum(select * gate[:, None, :], axis=2).reshape(slots, 1)
            gather = lambda table: jnp.einsum(
                "bct,btd->bcd", select, table, preferred_element_type=F32
            ).astype(BF).reshape(slots, D)
            combine = lambda made: jnp.einsum(
                "bct,bcd->btd",
                select,
                made.astype(BF).reshape(ways, capacity, D),
                preferred_element_type=F32,
            )
            sent = gather(routed_blocks)
            grad_sent_in = gather(grad_all)
            gate_pre = dot(sent, gate_full[j])
            up_pre = dot(sent, up_full[j])
            sigma = 1.0 / (1.0 + jnp.exp(-gate_pre))
            act = gate_pre * sigma * up_pre
            scaled = (act * slot_gate).astype(BF)
            made = dot(scaled, down_full[j])
            mixtures = add(mixtures, combine(made))
            lifted = dot_nt(grad_sent_in, down_full[j])
            row_dots = jnp.sum(act * lifted, axis=1).reshape(ways, capacity, 1)
            gate_grads.append(jnp.sum(select * row_dots, axis=1))
            grad_act = lifted * slot_gate
            grad_up = (grad_act * gate_pre * sigma).astype(BF)
            grad_gate = (grad_act * up_pre * sigma * (1.0 + gate_pre * (1.0 - sigma))).astype(BF)
            grad_in = dot_nt(grad_gate, gate_full[j]) + dot_nt(grad_up, up_full[j])
            grads_routed = add(grads_routed, combine(grad_in))
            backs.append((sent, grad_gate, grad_up, scaled, grad_sent_in))
        expert_rows.append(backs)
        mixtures = mixtures.astype(BF)
        grads_routed = grads_routed.astype(BF)
        mixture = collect([mixtures[b] for b in range(ways)], ways)
        result = ((hidden + mixture) * live_col).astype(BF)

        sends = jnp.stack(gate_grads, axis=1)
        sends = jnp.zeros_like(sends).at[sources].set(sends)
        gate_grad = lax.all_to_all(
            sends, "expert", split_axis=0, concat_axis=0, tiled=True
        ).reshape(experts, blk)
        own_gates = gates[:, 0]
        grad_logits = own_gates * (
            gate_grad - jnp.sum(own_gates * gate_grad, axis=0, keepdims=True)
        )
        grad_logits = grad_logits.astype(BF)
        grad_routed = collect([grads_routed[b] for b in range(ways)], ways)
        grad_routed = grad_routed + lax.dot_general(
            grad_logits, router, (((0,), (1,)), ((), ())), preferred_element_type=F32
        )
        g_router = add(
            g_router,
            lax.dot_general(
                routed, grad_logits, (((0,), (1,)), ((), ())), preferred_element_type=F32
            ),
        )
        g_ffn_gain = add(
            g_ffn_gain, jnp.sum(grad_routed * hidden * factor_ffn, axis=0, keepdims=True)
        )
        grad_hidden = grad_rows.astype(F32) * live_col + norm_back(
            grad_routed, hidden, factor_ffn, gain_ffn
        )

        gh_all = jnp.concatenate(spread(grad_hidden.astype(BF), chip, ways), axis=0)
        g_out_weight = add(g_out_weight, dot_tn(mixed, gh_all))
        grad_mixed = dot_nt(gh_all, w_out).astype(BF).reshape(ways, SEQ_MB, seg, hcols)
        g_qkv, head_gains = attend_back(qkv, grad_mixed, lse, cosine, sine, gains, keep)
        g_qkv = g_qkv.reshape(ways * blk, 3 * hcols)
        g_head_gains = add(g_head_gains, jnp.sum(head_gains, axis=0))
        g_qkv_weight = add(g_qkv_weight, dot_tn(normed, g_qkv))
        parts = dot_nt(g_qkv, w_qkv).astype(BF).reshape(ways, blk, D)
        grad_normed = collect([parts[b] for b in range(ways)], ways)
        grad_inputs = grad_hidden + norm_back(
            grad_normed, tokens_f32, norm_factor(tokens_f32), gain_in
        )
        for i, p in enumerate(picks):
            rows = slice(i * seg, (i + 1) * seg)
            outputs = lax.dynamic_update_index_in_dim(outputs, result[rows], p, 0)
            input_grads = lax.dynamic_update_index_in_dim(input_grads, grad_inputs[rows], p, 0)

    def expert_grad(left, right):
        full = jnp.stack(
            [
                sum(dot_tn(expert_rows[m][j][left], expert_rows[m][j][right]) for m in range(MICRO))
                for j in range(local)
            ]
        ).astype(BF)
        return lax.psum_scatter(full, "dp", scatter_dimension=1, tiled=True).astype(F32)

    grad_w_gate = expert_grad(0, 1)
    grad_w_up = expert_grad(0, 2)
    grad_w_down = expert_grad(3, 4)

    part = lax.psum_scatter(g_qkv_weight.astype(BF), "dp", scatter_dimension=0, tiled=True)
    part = lax.all_to_all(
        part.reshape(ways, own_rows, 3 * hcols), "expert", split_axis=0, concat_axis=0, tiled=True
    ).astype(F32)
    grad_q, grad_k, grad_v = (
        part[:, :, i * hcols : (i + 1) * hcols].transpose(1, 0, 2).reshape(own_rows, D)
        for i in range(3)
    )
    own_gain = attn_norm.astype(F32)
    grad_attn_norm = (
        jnp.sum(
            grad_q * query_weight.astype(F32)
            + grad_k * key_weight.astype(F32)
            + grad_v * value_weight.astype(F32),
            axis=1,
        )
        / own_gain
    )
    grad_out = lax.psum_scatter(g_out_weight.astype(BF), "dp", scatter_dimension=0, tiled=True)
    grad_out = lax.ppermute(grad_out, both, [(b, a) for a, b in owner_pairs]).astype(F32)

    tiled_gains = jnp.tile(g_head_gains.reshape(2, own_rows, -1), (1, dps * ways, 1))
    small_grads = jnp.concatenate(
        [g_router, g_ffn_gain.T, tiled_gains[0], tiled_gains[1]], axis=1
    )
    small_grads = lax.psum_scatter(small_grads, both, scatter_dimension=0, tiled=True)
    per = HEAD_WIDTH // own_rows
    return (
        outputs,
        input_grads,
        grad_attn_norm,
        grad_q,
        grad_k,
        grad_v,
        small_grads[:, experts + 1 : experts + 1 + per].reshape(HEAD_WIDTH),
        small_grads[:, experts + 1 + per :].reshape(HEAD_WIDTH),
        grad_out,
        small_grads[:, experts],
        small_grads[:, :experts],
        grad_w_gate,
        grad_w_up,
        grad_w_down,
    )


def solution(mesh):
    rows = P(("dp", "expert"), None)
    vector = P(("dp", "expert"))
    seqs = P("dp", "expert", None)
    weights = P("expert", "dp", None)
    return jax.shard_map(
        body,
        mesh=mesh,
        in_specs=(
            seqs,
            seqs,
            P("dp"),
            P("dp", None),
            seqs,
            vector,
            rows,
            rows,
            rows,
            P(),
            P(),
            rows,
            vector,
            rows,
            weights,
            weights,
            weights,
        ),
        out_specs=(
            seqs,
            seqs,
            vector,
            rows,
            rows,
            rows,
            P(),
            P(),
            rows,
            vector,
            rows,
            weights,
            weights,
            weights,
        ),
        check_vma=False,
    )
```

```python
import functools

import jax
import jax.numpy as jnp
from jax import lax
from jax.experimental import pallas as pl
from jax.experimental.pallas import tpu as pltpu
from jax.sharding import PartitionSpec as P

D = 2048
HEAD_COUNT = 16
HEAD_WIDTH = 128
TOP = 8
SEQ_MB = 2
MICRO = 2

EPS = 1e-06
NEG = -1e30
THETA = 10000.0
SCALE = HEAD_WIDTH ** (-0.5)
BF = jnp.bfloat16
F32 = jnp.float32


def dot(a, b):
    return lax.dot_general(a, b, (((1,), (0,)), ((), ())), preferred_element_type=F32)


def dot_nt(a, b):
    return lax.dot_general(a, b, (((1,), (1,)), ((), ())), preferred_element_type=F32)


def dot_tn(a, b):
    return lax.dot_general(a, b, (((0,), (0,)), ((), ())), preferred_element_type=F32)


def norm_factor(values):
    return lax.rsqrt(jnp.mean(values * values, axis=-1, keepdims=True) + EPS)


def norm_back(grad_after, rows, factor, gain):
    scaled = grad_after * gain
    shift = jnp.mean(scaled * rows, axis=-1, keepdims=True)
    return factor * scaled - rows * (factor * factor * factor * shift)


def swap_halves(values):
    return pltpu.roll(values, HEAD_WIDTH // 2, 1)


def head_columns(ref, index, length):
    cols = ref[:, 0, :, index * HEAD_WIDTH : (index + 1) * HEAD_WIDTH]
    return cols.reshape(length, HEAD_WIDTH)


def rotated(rows, gain, cosine, sine):
    factor = norm_factor(rows)
    normed = rows * factor * gain
    return (normed * cosine + swap_halves(normed) * sine).astype(BF), factor


def attend_kernel(
    place_ref, qkv_ref, cos_ref, sin_ref, gains_ref, keep_ref, mixed_ref, lse_ref, *, heads, tile
):
    blocks, _, seg, _ = qkv_ref.shape
    length = blocks * seg
    cosine = cos_ref[...]
    sine = sin_ref[...]
    keep = keep_ref[0] > 0
    for head in range(heads):
        q_rot, _ = rotated(head_columns(qkv_ref, head, length), gains_ref[0:1], cosine, sine)
        k_rot, _ = rotated(
            head_columns(qkv_ref, heads + head, length), gains_ref[1:2], cosine, sine
        )
        values = head_columns(qkv_ref, 2 * heads + head, length).astype(BF)
        for step in range(length // tile):
            rows = slice(step * tile, (step + 1) * tile)
            scores = jnp.where(keep, dot_nt(q_rot[rows], k_rot) * SCALE, NEG)
            peak = jnp.max(scores, axis=-1, keepdims=True)
            expo = jnp.exp(scores - peak)
            total = jnp.sum(expo, axis=-1, keepdims=True)
            mixed = dot((expo * (1.0 / total)).astype(BF), values)
            mixed = mixed.astype(BF)
            for sub in range(tile // seg):
                mixed_ref[
                    place_ref[step * tile // seg + sub],
                    0,
                    :,
                    head * HEAD_WIDTH : (head + 1) * HEAD_WIDTH,
                ] = mixed[sub * seg : (sub + 1) * seg]
            lse_ref[0, head, rows, :] = jnp.broadcast_to(
                peak + jnp.log(total), (tile, HEAD_WIDTH)
            )


def attend_back_kernel(
    place_ref,
    qkv_ref,
    grad_ref,
    lse_ref,
    cos_ref,
    sin_ref,
    gains_ref,
    keep_ref,
    out_ref,
    gain_ref,
    dq_ref,
    dk_ref,
    dv_ref,
    *,
    heads,
    tile,
):
    blocks, _, seg, _ = qkv_ref.shape
    length = blocks * seg
    cosine = cos_ref[...]
    sine = sin_ref[...]
    keep = keep_ref[0] > 0
    gain_sums = [jnp.zeros((1, HEAD_WIDTH), F32), jnp.zeros((1, HEAD_WIDTH), F32)]

    def store(index, rows):
        out_ref[:, 0, :, index * HEAD_WIDTH : (index + 1) * HEAD_WIDTH] = rows.astype(BF).reshape(
            blocks, seg, HEAD_WIDTH
        )

    for head in range(heads):
        q_rows = head_columns(qkv_ref, head, length)
        k_rows = head_columns(qkv_ref, heads + head, length)
        q_rot, q_factor = rotated(q_rows, gains_ref[0:1], cosine, sine)
        k_rot, k_factor = rotated(k_rows, gains_ref[1:2], cosine, sine)
        values = head_columns(qkv_ref, 2 * heads + head, length).astype(BF)
        grads = jnp.concatenate(
            [
                grad_ref[place_ref[b], 0, :, head * HEAD_WIDTH : (head + 1) * HEAD_WIDTH]
                for b in range(blocks)
            ],
            axis=0,
        )
        for step in range(length // tile):
            rows = slice(step * tile, (step + 1) * tile)
            scores = jnp.where(keep, dot_nt(q_rot[rows], k_rot) * SCALE, NEG)
            probs = jnp.exp(scores - lse_ref[0, head, rows, 0:1])
            grad_probs = dot_nt(grads[rows], values)
            inner = jnp.sum(probs * grad_probs, axis=-1, keepdims=True)
            grad_scores = (probs * (grad_probs - inner)).astype(BF)
            dq_ref[rows, :] = dot(grad_scores, k_rot) * SCALE
            dk = dot_tn(grad_scores, q_rot[rows])
            dv = dot_tn(probs.astype(BF), grads[rows])
            if step == 0:
                dk_ref[...] = dk
                dv_ref[...] = dv
            else:
                dk_ref[...] += dk
                dv_ref[...] += dv
        for which, (acc_ref, factor, source, scale) in enumerate(
            ((dq_ref, q_factor, q_rows, 1.0), (dk_ref, k_factor, k_rows, SCALE))
        ):
            grad = acc_ref[...] * scale
            grad = grad * cosine - swap_halves(grad) * sine
            gain_sums[which] += jnp.sum(grad * source * factor, axis=0, keepdims=True)
            store(
                which * heads + head,
                norm_back(grad, source, factor, gains_ref[which : which + 1]),
            )
        store(2 * heads + head, dv_ref[...])
    gain_ref[0] = jnp.concatenate(gain_sums, axis=0)


def attend(places, qkv, cosine, sine, gains, keep):
    blocks, seqs, seg, width = qkv.shape
    length = blocks * seg
    heads = width // (3 * HEAD_WIDTH)
    tile = max(length // 4, seg)
    full = lambda shape: pl.BlockSpec(shape, lambda s: (0,) * len(shape))
    return pl.pallas_call(
        functools.partial(attend_kernel, heads=heads, tile=tile),
        grid=(seqs,),
        in_specs=[
            pl.BlockSpec(memory_space=pltpu.SMEM),
            pl.BlockSpec((blocks, 1, seg, width), lambda s: (0, s, 0, 0)),
            full((length, HEAD_WIDTH)),
            full((length, HEAD_WIDTH)),
            full((2, HEAD_WIDTH)),
            pl.BlockSpec((1, 1, length), lambda s: (s, 0, 0)),
        ],
        out_specs=[
            pl.BlockSpec((blocks, 1, seg, heads * HEAD_WIDTH), lambda s: (0, s, 0, 0)),
            pl.BlockSpec((1, heads, length, HEAD_WIDTH), lambda s: (s, 0, 0, 0)),
        ],
        out_shape=[
            jax.ShapeDtypeStruct((blocks, seqs, seg, heads * HEAD_WIDTH), BF),
            jax.ShapeDtypeStruct((seqs, heads, length, HEAD_WIDTH), F32),
        ],
        name="attend",
    )(places, qkv, cosine, sine, gains, keep)


def attend_back(places, qkv, grads, lse, cosine, sine, gains, keep):
    blocks, seqs, seg, width = qkv.shape
    length = blocks * seg
    heads = width // (3 * HEAD_WIDTH)
    tile = max(length // 4, seg)
    full = lambda shape: pl.BlockSpec(shape, lambda s: (0,) * len(shape))
    return pl.pallas_call(
        functools.partial(attend_back_kernel, heads=heads, tile=tile),
        grid=(seqs,),
        in_specs=[
            pl.BlockSpec(memory_space=pltpu.SMEM),
            pl.BlockSpec((blocks, 1, seg, width), lambda s: (0, s, 0, 0)),
            pl.BlockSpec((blocks, 1, seg, heads * HEAD_WIDTH), lambda s: (0, s, 0, 0)),
            pl.BlockSpec((1, heads, length, HEAD_WIDTH), lambda s: (s, 0, 0, 0)),
            full((length, HEAD_WIDTH)),
            full((length, HEAD_WIDTH)),
            full((2, HEAD_WIDTH)),
            pl.BlockSpec((1, 1, length), lambda s: (s, 0, 0)),
        ],
        out_specs=[
            pl.BlockSpec((blocks, 1, seg, width), lambda s: (0, s, 0, 0)),
            pl.BlockSpec((1, 2, HEAD_WIDTH), lambda s: (s, 0, 0)),
        ],
        out_shape=[
            jax.ShapeDtypeStruct((blocks, seqs, seg, width), BF),
            jax.ShapeDtypeStruct((seqs, 2, HEAD_WIDTH), F32),
        ],
        scratch_shapes=[pltpu.VMEM((length, HEAD_WIDTH), F32)] * 3,
        name="attend_back",
    )(places, qkv, grads, lse, cosine, sine, gains, keep)


def rotate(value, ways, move):
    chips = ways // 2
    pairs = [(2 * s + k, 2 * ((s + move) % chips) + k) for s in range(chips) for k in (0, 1)]
    return lax.ppermute(value, "expert", pairs)


def exchange(value, ways):
    return lax.ppermute(value, "expert", [(e, e ^ 1) for e in range(ways)])


def column(block, ways):
    return [block] + [rotate(block, ways, h) for h in range(1, ways // 2)]


def partners(blocks, ways):
    return [exchange(value, ways) for value in blocks]


def pair_up(parts, ways):
    chips = ways // 2
    other = exchange(parts[chips:], ways)
    own = parts[0].astype(F32) + other[0].astype(F32)
    rest = [
        (parts[h].astype(F32) + other[h].astype(F32)).astype(BF) for h in range(1, chips)
    ]
    return lax.optimization_barrier((own, *rest))


def deliver(rest, ways, *earlier):
    return [rotate(after(part, *earlier), ways, -(h + 1)) for h, part in enumerate(rest)]


def total_of(own, arrived):
    for part in arrived:
        own = own + part.astype(F32)
    return own


def after(value, *earlier):
    return lax.optimization_barrier((value,) + earlier)[0]


def take_major(array, index):
    return lax.dynamic_index_in_dim(array, index, 0, keepdims=False)


def body(
    tokens,
    cotangent,
    lengths,
    order,
    routes,
    attn_norm,
    query_weight,
    key_weight,
    value_weight,
    q_norm,
    k_norm,
    output_weight,
    ffn_norm,
    w_router,
    w_gate,
    w_up,
    w_down,
):
    both = ("dp", "expert")
    dps = lax.axis_size("dp")
    ways = lax.axis_size("expert")
    chips = ways // 2
    me = lax.axis_index("expert")
    chip, core = me // 2, me % 2
    seqs, seg, _ = tokens.shape
    length = seg * ways
    blk = SEQ_MB * seg
    own_rows = attn_norm.shape[0]
    experts = w_router.shape[1]
    capacity = blk * TOP // experts
    local = w_gate.shape[0]
    ff = w_gate.shape[2]
    hcols = D // ways
    slots = ways * capacity

    sources = jnp.stack(
        [((chip + chips - h) % chips) * 2 + (core ^ cc) for cc in (0, 1) for h in range(chips)]
    )
    positions = (sources[:, None] * seg + jnp.arange(seg, dtype=jnp.int32)[None, :]).reshape(length)
    inverse = THETA ** (-(2.0 * jnp.arange(HEAD_WIDTH // 2, dtype=F32)) / HEAD_WIDTH)
    angles = positions.astype(F32)[:, None] * inverse[None, :]
    cosine = jnp.concatenate([jnp.cos(angles)] * 2, axis=1)
    sine = jnp.concatenate([-jnp.sin(angles), jnp.sin(angles)], axis=1)
    gains = jnp.stack([q_norm, k_norm]).astype(F32)

    own_gain = attn_norm.astype(F32)[:, None]
    split = lambda weight: (weight.astype(F32) * own_gain).astype(BF).reshape(own_rows, ways, hcols)
    qkv_part = jnp.concatenate(
        [split(query_weight), split(key_weight), split(value_weight)], axis=2
    ).transpose(1, 0, 2)
    qkv_part = lax.all_to_all(qkv_part, "expert", split_axis=0, concat_axis=0, tiled=True)
    w_qkv = lax.all_gather(
        qkv_part.reshape(ways * own_rows, 3 * hcols), "dp", axis=0, tiled=True
    )

    route_cols = routes.astype(BF).reshape(own_rows, -1)
    small = jnp.concatenate([w_router, ffn_norm[:, None], route_cols], axis=1)
    route_end = small.shape[1]
    small = jnp.pad(small, ((0, 0), (0, -route_end % 128)))
    small = lax.all_gather(
        jnp.concatenate([output_weight, small], axis=1), both, axis=0, tiled=True
    )
    w_out, small = small[:, :D], small[:, D:]
    router = small[:, :experts]
    gain_ffn = small[:, experts].astype(F32)[None, :]
    all_routes = lax.dynamic_index_in_dim(
        small[:, experts + 1 : route_end].reshape(dps, ways, own_rows, -1),
        lax.axis_index("dp"),
        0,
        keepdims=False,
    ).reshape(ways, seqs, seg, TOP)
    all_routes = jnp.take(all_routes, sources, axis=0).transpose(1, 0, 3, 2)

    gate_full = lax.all_gather(w_gate, "dp", axis=1, tiled=True)
    up_full = lax.all_gather(w_up, "dp", axis=1, tiled=True)
    down_full = lax.all_gather(w_down, "dp", axis=1, tiled=True)

    strict = (
        jnp.arange(blk, dtype=jnp.int32)[:, None] < jnp.arange(blk, dtype=jnp.int32)[None, :]
    ).astype(BF)
    slot_ids = jnp.arange(capacity, dtype=jnp.int32)[None, :, None]
    expert_ids = jnp.arange(experts, dtype=jnp.int32)

    def add(total, part):
        return part if total is None else total + part

    def rows_of(array, picks):
        return jnp.concatenate([take_major(array, p) for p in picks], axis=0)

    def attention(s, gathered, *earlier):
        normed = jnp.concatenate(
            [
                (b * norm_factor(b)).astype(BF)
                for b in (block.astype(F32) for block in gathered)
            ],
            axis=0,
        )
        qkv = after(dot(normed, w_qkv), *earlier).reshape(ways, SEQ_MB, seg, 3 * hcols)
        mixed, lse = attend(sources, qkv, cosine, sine, gains, s["keep"])
        s.update(normed=normed, qkv=qkv, lse=lse, mixed_heads=mixed)

    def projection(s):
        mixed = lax.all_to_all(
            s["mixed_heads"], "expert", split_axis=0, concat_axis=0, tiled=True
        )
        mixed = mixed.transpose(1, 2, 0, 3).reshape(blk, D)
        hidden = s["rows"].astype(F32) + dot(mixed, w_out)
        factor_ffn = norm_factor(hidden)
        routed = (hidden * factor_ffn * gain_ffn).astype(BF)
        s.update(mixed=mixed, hidden=hidden, factor_ffn=factor_ffn, routed=routed)

    def expert_layer(s, routed_all, grad_all, waits):
        routed_blocks = routed_all.reshape(ways, blk, D)
        picked = jnp.stack([take_major(all_routes, p) for p in s["picks"]], axis=2)
        picked = picked.reshape(ways, TOP, blk).astype(jnp.int32)
        alive = s["live_at"].reshape(SEQ_MB, ways, seg).transpose(1, 0, 2).reshape(ways, blk)
        logits = lax.dot_general(
            router, routed_all, (((0,), (1,)), ((), ())), preferred_element_type=F32
        ).reshape(experts, ways, blk)
        chosen = jnp.any(picked[None] == expert_ids[:, None, None, None], axis=2)
        masked = jnp.where(chosen, logits, NEG)
        expo = jnp.exp(masked - jnp.max(masked, axis=0, keepdims=True))
        gates = expo / jnp.sum(expo, axis=0, keepdims=True)
        backs = []
        pin = lambda value, name, j: after(value, *waits.get((name, j), tuple)())
        mixtures = grads_routed = None
        gate_grads = []
        for j in range(local):
            mine = me * local + j
            hits = jnp.any(picked == mine, axis=1) & alive
            rank = dot(hits.astype(BF), strict).astype(jnp.int32)
            select = ((rank[:, None, :] == slot_ids) & hits[:, None, :]).astype(BF)
            gate = take_major(gates, mine)
            slot_gate = jnp.sum(select * gate[:, None, :], axis=2).reshape(slots, 1)
            gather = lambda table: jnp.einsum(
                "bct,btd->bcd", select, table, preferred_element_type=F32
            ).astype(BF).reshape(slots, D)
            combine = lambda made: jnp.einsum(
                "bct,bcd->btd",
                select,
                made.reshape(ways, capacity, D),
                preferred_element_type=F32,
            )
            sent = gather(pin(routed_blocks, "sent", j))
            grad_sent_in = gather(grad_all.reshape(ways, blk, D))
            gate_pre = dot(sent, gate_full[j])
            up_pre = dot(sent, up_full[j])
            sigma = 1.0 / (1.0 + jnp.exp(-gate_pre))
            act = gate_pre * sigma * up_pre
            scaled = (act * slot_gate).astype(BF)
            made = dot(scaled, down_full[j])
            mixtures = add(mixtures, combine(pin(made.astype(BF), "made", j)))
            lifted = dot_nt(grad_sent_in, down_full[j])
            row_dots = jnp.sum(act * lifted, axis=1).reshape(ways, capacity, 1)
            gate_grads.append(jnp.sum(select * row_dots, axis=1))
            grad_act = pin(lifted, "lifted", j) * slot_gate
            grad_up = (grad_act * gate_pre * sigma).astype(BF)
            grad_gate = (grad_act * up_pre * sigma * (1.0 + gate_pre * (1.0 - sigma))).astype(BF)
            grad_in = dot_nt(grad_gate, gate_full[j]) + dot_nt(grad_up, up_full[j])
            grads_routed = add(grads_routed, combine(pin(grad_in.astype(BF), "grad_in", j)))
            backs.append((sent, grad_gate, grad_up, scaled, grad_sent_in))
            s.setdefault("partial", grads_routed)
        s.update(
            backs=backs,
            gates=gates[:, 0],
            gate_grads=jnp.stack(gate_grads, axis=1),
            mixtures=mixtures.astype(BF),
            grads_routed=grads_routed.astype(BF),
        )

    def token_backward(s):
        sends = jnp.zeros_like(s["gate_grads"]).at[sources].set(s["gate_grads"])
        gate_grad = lax.all_to_all(
            sends, "expert", split_axis=0, concat_axis=0, tiled=True
        ).reshape(experts, blk)
        own_gates = s["gates"]
        grad_logits = own_gates * (
            gate_grad - jnp.sum(own_gates * gate_grad, axis=0, keepdims=True)
        )
        grad_logits = grad_logits.astype(BF)
        grad_routed = total_of(s["pair_g"][0], s["arrived_g"]) + lax.dot_general(
            grad_logits, router, (((0,), (1,)), ((), ())), preferred_element_type=F32
        )
        s["g_router"] = lax.dot_general(
            s["routed"], grad_logits, (((0,), (1,)), ((), ())), preferred_element_type=F32
        )
        hidden, factor_ffn = s["hidden"], s["factor_ffn"]
        s["g_ffn_gain"] = jnp.sum(grad_routed * hidden * factor_ffn, axis=0, keepdims=True)
        grad_hidden = s["grad_rows"].astype(F32) * s["live_col"] + norm_back(
            grad_routed, hidden, factor_ffn, gain_ffn
        )
        gh = grad_hidden.astype(BF)
        grad_mixed = dot_nt(gh, w_out).astype(BF).reshape(SEQ_MB, seg, ways, hcols)
        grad_mixed = grad_mixed.transpose(2, 0, 1, 3)
        s.update(grad_hidden=grad_hidden, gh=gh, grad_send=grad_mixed)
        s["grad_mixed"] = lax.all_to_all(
            grad_mixed, "expert", split_axis=0, concat_axis=0, tiled=True
        )

    def attention_backward(s, first, second):
        g_qkv, head_gains = attend_back(
            sources, s["qkv"], after(s["grad_mixed"], *first), s["lse"], cosine, sine, gains, s["keep"]
        )
        s["g_qkv"] = g_qkv.reshape(ways * blk, 3 * hcols)
        s["g_head_gains"] = jnp.sum(head_gains, axis=0)
        g_rows = after(s["g_qkv"], *second())
        s["parts"] = dot_nt(g_rows, w_qkv).astype(BF).reshape(ways, blk, D)

    def expert_grad(left, right, *earlier):
        full = jnp.stack(
            [
                sum(
                    dot_tn(after(s["backs"][j][left], *earlier), s["backs"][j][right])
                    for s in state
                )
                for j in range(local)
            ]
        ).astype(BF)
        return full, lax.psum_scatter(full, "dp", scatter_dimension=1, tiled=True)

    state = []
    for micro in range(MICRO):
        picks = [order[0, micro * SEQ_MB + i] for i in range(SEQ_MB)]
        seq_lens = jnp.stack([lengths[p] for p in picks])
        live_at = positions[None, :] < seq_lens[:, None]
        state.append(
            dict(
                picks=picks,
                live_at=live_at,
                keep=live_at.astype(F32)[:, None, :],
                live_col=live_at.reshape(SEQ_MB, ways, seg)[:, 0].reshape(blk, 1).astype(F32),
                rows=rows_of(tokens, picks),
                grad_rows=rows_of(cotangent, picks),
            )
        )

    one, two = state
    tokens_one = column(one["rows"], ways)
    tokens_two = column(two["rows"], ways)
    attention(one, tokens_one + partners(tokens_one, ways), tokens_two[1])
    tokens_two = [after(block, one["mixed_heads"]) for block in tokens_two]
    tokens_two = tokens_two + partners(tokens_two, ways)
    projection(one)
    routed_one = column(after(one["routed"], *tokens_two[1 : ways // 2]), ways)
    attention(two, [after(block, one["routed"]) for block in tokens_two])
    routed_one = [after(block, two["mixed_heads"]) for block in routed_one]
    grads_one = column(after(one["grad_rows"], *routed_one[1:]), ways)
    routed_one = routed_one + partners(routed_one, ways)
    projection(two)
    routed_two = column(after(two["routed"], *grads_one[1:]), ways)
    grads_one = grads_one + partners(grads_one, ways)
    grads_two = column(after(two["grad_rows"], *routed_two[1:]), ways)
    merge = lambda blocks: jnp.concatenate(blocks, axis=0)

    expert_layer(
        one,
        after(merge(routed_one), two["routed"]),
        merge(grads_one),
        {
            ("sent", local - 1): lambda: tuple(routed_two[1:]),
            ("made", local - 1): lambda: tuple(grads_two[1:]),
        },
    )
    routed_two = [after(block, one["partial"]) for block in routed_two]
    routed_two = routed_two + partners(routed_two, ways)
    grads_two = grads_two + partners(grads_two, ways)

    one["pair_g"] = pair_up(one["grads_routed"], ways)
    one["arrived_g"] = deliver(one["pair_g"][1:], ways, *grads_two[1 : ways // 2])
    one["pair_m"] = pair_up(one["mixtures"], ways)
    one["arrived_m"] = deliver(one["pair_m"][1:], ways, *one["arrived_g"])
    expert_layer(
        two,
        after(merge(routed_two), one["mixtures"], one["grads_routed"]),
        merge(grads_two),
        {
            ("lifted", 0): lambda: tuple(one["pair_g"]) + tuple(one["pair_m"]),
            ("grad_in", local - 1): lambda: tuple(one["arrived_g"]),
        },
    )
    one["arrived_m"] = [after(part, two["grads_routed"]) for part in one["arrived_m"]]
    two["pair_g"] = pair_up(two["grads_routed"], ways)
    two["arrived_g"] = deliver(two["pair_g"][1:], ways, *one["arrived_m"])
    one["arrived_g"] = [after(part, two["grads_routed"]) for part in one["arrived_g"]]
    token_backward(one)
    full_gate, grad_w_gate = expert_grad(0, 1, one["grad_send"])
    full_up, grad_w_up = expert_grad(
        0, 2, full_gate, one["grad_mixed"], *two["pair_g"], *one["arrived_m"]
    )
    two["pair_m"] = pair_up(two["mixtures"], ways)
    full_down, grad_w_down = expert_grad(3, 4, full_up, *two["pair_m"])
    two["arrived_m"] = deliver(two["pair_m"][1:], ways, *two["arrived_g"])
    two["arrived_g"] = [after(part, full_down) for part in two["arrived_g"]]
    token_backward(two)
    attention_backward(one, (two["grad_send"], grad_w_gate), lambda: ())
    two["arrived_m"] = [after(part, one["g_qkv"]) for part in two["arrived_m"]]
    one["pair_p"] = pair_up(one["parts"], ways)
    g_out_weight = dot_tn(
        after(jnp.concatenate([s["mixed"] for s in state], axis=0), one["g_qkv"]),
        jnp.concatenate([s["gh"] for s in state], axis=0),
    )
    one["arrived_p"] = deliver(one["pair_p"][1:], ways, *two["arrived_m"])
    attention_backward(
        two,
        (g_out_weight, grad_w_up) + tuple(one["pair_p"]) + tuple(two["arrived_m"]),
        lambda: (),
    )
    two["pair_p"] = pair_up(two["parts"], ways)
    two["arrived_p"] = deliver(two["pair_p"][1:], ways, *one["arrived_p"])
    g_qkv_weight = sum(
        dot_tn(after(s["normed"], grad_w_down, *two["pair_p"], *one["arrived_p"]), s["g_qkv"])
        for s in state
    )
    g_router = sum(s["g_router"] for s in state)
    g_ffn_gain = sum(s["g_ffn_gain"] for s in state)
    g_head_gains = sum(s["g_head_gains"] for s in state)

    outputs = jnp.zeros(tokens.shape, BF)
    input_grads = jnp.zeros(tokens.shape, F32)
    for s in state:
        result = (
            (s["hidden"] + total_of(s["pair_m"][0], s["arrived_m"])) * s["live_col"]
        ).astype(BF)
        tokens_f32 = s["rows"].astype(F32)
        grad_inputs = s["grad_hidden"] + norm_back(
            total_of(s["pair_p"][0], s["arrived_p"]), tokens_f32, norm_factor(tokens_f32), 1.0
        )
        for i, p in enumerate(s["picks"]):
            rows = slice(i * seg, (i + 1) * seg)
            outputs = lax.dynamic_update_index_in_dim(outputs, result[rows], p, 0)
            input_grads = lax.dynamic_update_index_in_dim(input_grads, grad_inputs[rows], p, 0)

    split_own = lambda weight: weight.astype(F32).reshape(own_rows, ways, hcols).transpose(1, 0, 2)
    part = lax.psum_scatter(g_qkv_weight.astype(BF), "dp", scatter_dimension=0, tiled=True)
    part = lax.all_to_all(
        part.reshape(ways, own_rows, 3 * hcols), "expert", split_axis=0, concat_axis=0, tiled=True
    ).astype(F32)
    plain = jnp.sum(
        part[:, :, :hcols] * split_own(query_weight)
        + part[:, :, hcols : 2 * hcols] * split_own(key_weight)
        + part[:, :, 2 * hcols :] * split_own(value_weight),
        axis=(0, 2),
    )
    grad_q, grad_k, grad_v = (
        part[:, :, i * hcols : (i + 1) * hcols].transpose(1, 0, 2).reshape(own_rows, D) * own_gain
        for i in range(3)
    )
    grad_attn_norm = plain
    out_part = lax.psum_scatter(
        g_out_weight.astype(BF), "dp", scatter_dimension=0, tiled=True
    ).reshape(ways, own_rows, D)
    out_pair = pair_up(jnp.take(out_part, sources, axis=0), ways)
    grad_out = total_of(out_pair[0], deliver(out_pair[1:], ways))

    tiled_gains = jnp.tile(g_head_gains.reshape(2, own_rows, -1), (1, dps * ways, 1))
    small_grads = jnp.concatenate(
        [g_router, g_ffn_gain.T, tiled_gains[0], tiled_gains[1]], axis=1
    )
    small_grads = lax.psum_scatter(small_grads, both, scatter_dimension=0, tiled=True)
    per = HEAD_WIDTH // own_rows
    return (
        outputs,
        input_grads,
        grad_attn_norm,
        grad_q,
        grad_k,
        grad_v,
        small_grads[:, experts + 1 : experts + 1 + per].reshape(HEAD_WIDTH),
        small_grads[:, experts + 1 + per :].reshape(HEAD_WIDTH),
        grad_out,
        small_grads[:, experts],
        small_grads[:, :experts],
        grad_w_gate.astype(F32),
        grad_w_up.astype(F32),
        grad_w_down.astype(F32),
    )


def solution(mesh):
    rows = P(("dp", "expert"), None)
    vector = P(("dp", "expert"))
    seqs = P("dp", "expert", None)
    weights = P("expert", "dp", None)
    return jax.shard_map(
        body,
        mesh=mesh,
        in_specs=(
            seqs,
            seqs,
            P("dp"),
            P("dp", None),
            seqs,
            vector,
            rows,
            rows,
            rows,
            P(),
            P(),
            rows,
            vector,
            rows,
            weights,
            weights,
            weights,
        ),
        out_specs=(
            seqs,
            seqs,
            vector,
            rows,
            rows,
            rows,
            P(),
            P(),
            rows,
            vector,
            rows,
            weights,
            weights,
            weights,
        ),
        check_vma=False,
    )
```

```python
import functools
from types import SimpleNamespace

import jax
import jax.numpy as jnp
from jax import lax
from jax.experimental import pallas as pl
from jax.experimental.pallas import tpu as pltpu
from jax.sharding import PartitionSpec as P

D = 2048
HEAD_COUNT = 16
HEAD_WIDTH = 128
TOP = 8
SEQ_MB = 2
MICRO = 2

EPS = 1e-06
NEG = -1e30
THETA = 10000.0
SCALE = HEAD_WIDTH ** (-0.5)
BF = jnp.bfloat16
F32 = jnp.float32


def dot(a, b):
    return lax.dot_general(a, b, (((1,), (0,)), ((), ())), preferred_element_type=F32)


def dot_nt(a, b):
    return lax.dot_general(a, b, (((1,), (1,)), ((), ())), preferred_element_type=F32)


def dot_tn(a, b):
    return lax.dot_general(a, b, (((0,), (0,)), ((), ())), preferred_element_type=F32)


def norm_factor(values):
    return lax.rsqrt(jnp.mean(values * values, axis=-1, keepdims=True) + EPS)


def norm_back(grad_after, rows, factor, gain):
    scaled = grad_after * gain
    shift = jnp.mean(scaled * rows, axis=-1, keepdims=True)
    return factor * scaled - rows * (factor * factor * factor * shift)


def swap_halves(values):
    return pltpu.roll(values, HEAD_WIDTH // 2, 1)


def head_columns(ref, index, length):
    cols = ref[:, 0, :, index * HEAD_WIDTH : (index + 1) * HEAD_WIDTH]
    return cols.reshape(length, HEAD_WIDTH)


def rotated(rows, gain, cosine, sine):
    factor = norm_factor(rows)
    normed = rows * factor * gain
    return (normed * cosine + swap_halves(normed) * sine).astype(BF), factor


def attend_kernel(
    place_ref, qkv_ref, cos_ref, sin_ref, gains_ref, keep_ref, mixed_ref, lse_ref, *, heads, tile
):
    blocks, _, seg, _ = qkv_ref.shape
    length = blocks * seg
    cosine = cos_ref[...]
    sine = sin_ref[...]
    keep = keep_ref[0] > 0
    for head in range(heads):
        q_rot, _ = rotated(head_columns(qkv_ref, head, length), gains_ref[0:1], cosine, sine)
        k_rot, _ = rotated(
            head_columns(qkv_ref, heads + head, length), gains_ref[1:2], cosine, sine
        )
        values = head_columns(qkv_ref, 2 * heads + head, length).astype(BF)
        for step in range(length // tile):
            rows = slice(step * tile, (step + 1) * tile)
            scores = jnp.where(keep, dot_nt(q_rot[rows], k_rot) * SCALE, NEG)
            peak = jnp.max(scores, axis=-1, keepdims=True)
            expo = jnp.exp(scores - peak)
            total = jnp.sum(expo, axis=-1, keepdims=True)
            mixed = dot((expo * (1.0 / total)).astype(BF), values)
            mixed = mixed.astype(BF)
            for sub in range(tile // seg):
                mixed_ref[
                    place_ref[step * tile // seg + sub],
                    0,
                    :,
                    head * HEAD_WIDTH : (head + 1) * HEAD_WIDTH,
                ] = mixed[sub * seg : (sub + 1) * seg]
            lse_ref[0, head, rows, :] = jnp.broadcast_to(
                peak + jnp.log(total), (tile, HEAD_WIDTH)
            )


def attend_back_kernel(
    place_ref,
    qkv_ref,
    grad_ref,
    lse_ref,
    cos_ref,
    sin_ref,
    gains_ref,
    keep_ref,
    out_ref,
    gain_ref,
    dq_ref,
    dk_ref,
    dv_ref,
    *,
    heads,
    tile,
):
    blocks, _, seg, _ = qkv_ref.shape
    length = blocks * seg
    cosine = cos_ref[...]
    sine = sin_ref[...]
    keep = keep_ref[0] > 0
    gain_sums = [jnp.zeros((1, HEAD_WIDTH), F32), jnp.zeros((1, HEAD_WIDTH), F32)]

    def store(index, rows):
        out_ref[:, 0, :, index * HEAD_WIDTH : (index + 1) * HEAD_WIDTH] = rows.astype(BF).reshape(
            blocks, seg, HEAD_WIDTH
        )

    for head in range(heads):
        q_rows = head_columns(qkv_ref, head, length)
        k_rows = head_columns(qkv_ref, heads + head, length)
        q_rot, q_factor = rotated(q_rows, gains_ref[0:1], cosine, sine)
        k_rot, k_factor = rotated(k_rows, gains_ref[1:2], cosine, sine)
        values = head_columns(qkv_ref, 2 * heads + head, length).astype(BF)
        grads = jnp.concatenate(
            [
                grad_ref[place_ref[b], 0, :, head * HEAD_WIDTH : (head + 1) * HEAD_WIDTH]
                for b in range(blocks)
            ],
            axis=0,
        )
        for step in range(length // tile):
            rows = slice(step * tile, (step + 1) * tile)
            scores = jnp.where(keep, dot_nt(q_rot[rows], k_rot) * SCALE, NEG)
            probs = jnp.exp(scores - lse_ref[0, head, rows, 0:1])
            grad_probs = dot_nt(grads[rows], values)
            inner = jnp.sum(probs * grad_probs, axis=-1, keepdims=True)
            grad_scores = (probs * (grad_probs - inner)).astype(BF)
            dq_ref[rows, :] = dot(grad_scores, k_rot) * SCALE
            dk = dot_tn(grad_scores, q_rot[rows])
            dv = dot_tn(probs.astype(BF), grads[rows])
            if step == 0:
                dk_ref[...] = dk
                dv_ref[...] = dv
            else:
                dk_ref[...] += dk
                dv_ref[...] += dv
        for which, (acc_ref, factor, source, scale) in enumerate(
            ((dq_ref, q_factor, q_rows, 1.0), (dk_ref, k_factor, k_rows, SCALE))
        ):
            grad = acc_ref[...] * scale
            grad = grad * cosine - swap_halves(grad) * sine
            gain_sums[which] += jnp.sum(grad * source * factor, axis=0, keepdims=True)
            store(
                which * heads + head,
                norm_back(grad, source, factor, gains_ref[which : which + 1]),
            )
        store(2 * heads + head, dv_ref[...])
    gain_ref[0] = jnp.concatenate(gain_sums, axis=0)


def attend(places, qkv, cosine, sine, gains, keep):
    blocks, seqs, seg, width = qkv.shape
    length = blocks * seg
    heads = width // (3 * HEAD_WIDTH)
    tile = max(length // 4, seg)
    full = lambda shape: pl.BlockSpec(shape, lambda s: (0,) * len(shape))
    return pl.pallas_call(
        functools.partial(attend_kernel, heads=heads, tile=tile),
        grid=(seqs,),
        in_specs=[
            pl.BlockSpec(memory_space=pltpu.SMEM),
            pl.BlockSpec((blocks, 1, seg, width), lambda s: (0, s, 0, 0)),
            full((length, HEAD_WIDTH)),
            full((length, HEAD_WIDTH)),
            full((2, HEAD_WIDTH)),
            pl.BlockSpec((1, 1, length), lambda s: (s, 0, 0)),
        ],
        out_specs=[
            pl.BlockSpec((blocks, 1, seg, heads * HEAD_WIDTH), lambda s: (0, s, 0, 0)),
            pl.BlockSpec((1, heads, length, HEAD_WIDTH), lambda s: (s, 0, 0, 0)),
        ],
        out_shape=[
            jax.ShapeDtypeStruct((blocks, seqs, seg, heads * HEAD_WIDTH), BF),
            jax.ShapeDtypeStruct((seqs, heads, length, HEAD_WIDTH), F32),
        ],
        name="attend",
    )(places, qkv, cosine, sine, gains, keep)


def attend_back(places, qkv, grads, lse, cosine, sine, gains, keep):
    blocks, seqs, seg, width = qkv.shape
    length = blocks * seg
    heads = width // (3 * HEAD_WIDTH)
    tile = max(length // 4, seg)
    full = lambda shape: pl.BlockSpec(shape, lambda s: (0,) * len(shape))
    return pl.pallas_call(
        functools.partial(attend_back_kernel, heads=heads, tile=tile),
        grid=(seqs,),
        in_specs=[
            pl.BlockSpec(memory_space=pltpu.SMEM),
            pl.BlockSpec((blocks, 1, seg, width), lambda s: (0, s, 0, 0)),
            pl.BlockSpec((blocks, 1, seg, heads * HEAD_WIDTH), lambda s: (0, s, 0, 0)),
            pl.BlockSpec((1, heads, length, HEAD_WIDTH), lambda s: (s, 0, 0, 0)),
            full((length, HEAD_WIDTH)),
            full((length, HEAD_WIDTH)),
            full((2, HEAD_WIDTH)),
            pl.BlockSpec((1, 1, length), lambda s: (s, 0, 0)),
        ],
        out_specs=[
            pl.BlockSpec((blocks, 1, seg, width), lambda s: (0, s, 0, 0)),
            pl.BlockSpec((1, 2, HEAD_WIDTH), lambda s: (s, 0, 0)),
        ],
        out_shape=[
            jax.ShapeDtypeStruct((blocks, seqs, seg, width), BF),
            jax.ShapeDtypeStruct((seqs, 2, HEAD_WIDTH), F32),
        ],
        scratch_shapes=[pltpu.VMEM((length, HEAD_WIDTH), F32)] * 3,
        name="attend_back",
    )(places, qkv, grads, lse, cosine, sine, gains, keep)


def rotate(value, ways, move):
    chips = ways // 2
    pairs = [(2 * s + k, 2 * ((s + move) % chips) + k) for s in range(chips) for k in (0, 1)]
    return lax.ppermute(value, "expert", pairs)


def exchange(value, ways):
    return lax.ppermute(value, "expert", [(e, e ^ 1) for e in range(ways)])


def column(block, ways):
    return [block] + [rotate(block, ways, h) for h in range(1, ways // 2)]


def partners(blocks, ways):
    return [exchange(value, ways) for value in blocks]


def pair_up(parts, sources, ways):
    chips = ways // 2
    mine = [take_major(parts, sources[h]) for h in range(chips)]
    other = exchange(jnp.stack([take_major(parts, sources[chips + h]) for h in range(chips)]), ways)
    own = mine[0].astype(F32) + other[0].astype(F32)
    rest = [(mine[h].astype(F32) + other[h].astype(F32)).astype(BF) for h in range(1, chips)]
    return lax.optimization_barrier((own, *rest))


def in_order(blocks, sources):
    whole = jnp.zeros((len(blocks),) + blocks[0].shape, blocks[0].dtype)
    for place, block in enumerate(blocks):
        whole = lax.dynamic_update_index_in_dim(whole, block, sources[place], 0)
    return whole.reshape((-1,) + blocks[0].shape[1:])


def deliver(rest, ways, *earlier):
    return [rotate(after(part, *earlier), ways, -(h + 1)) for h, part in enumerate(rest)]


def total_of(own, arrived):
    for part in arrived:
        own = own + part.astype(F32)
    return own


def after(value, *earlier):
    return lax.optimization_barrier((value,) + earlier)[0]


def take_major(array, index):
    return lax.dynamic_index_in_dim(array, index, 0, keepdims=False)


def body(
    tokens,
    cotangent,
    lengths,
    order,
    routes,
    attn_norm,
    query_weight,
    key_weight,
    value_weight,
    q_norm,
    k_norm,
    output_weight,
    ffn_norm,
    w_router,
    w_gate,
    w_up,
    w_down,
):
    both = ("dp", "expert")
    dps = lax.axis_size("dp")
    ways = lax.axis_size("expert")
    chips = ways // 2
    me = lax.axis_index("expert")
    chip, core = me // 2, me % 2
    seqs, seg, _ = tokens.shape
    length = seg * ways
    blk = SEQ_MB * seg
    own_rows = attn_norm.shape[0]
    experts = w_router.shape[1]
    capacity = blk * TOP // experts
    local = w_gate.shape[0]
    ff = w_gate.shape[2]
    hcols = D // ways
    slots = ways * capacity

    sources = jnp.stack(
        [((chip + chips - h) % chips) * 2 + (core ^ cc) for cc in (0, 1) for h in range(chips)]
    )
    positions = jnp.arange(length, dtype=jnp.int32)
    places = jnp.arange(ways, dtype=jnp.int32)
    inverse = THETA ** (-(2.0 * jnp.arange(HEAD_WIDTH // 2, dtype=F32)) / HEAD_WIDTH)
    angles = positions.astype(F32)[:, None] * inverse[None, :]
    cosine = jnp.concatenate([jnp.cos(angles)] * 2, axis=1)
    sine = jnp.concatenate([-jnp.sin(angles), jnp.sin(angles)], axis=1)
    gains = jnp.stack([q_norm, k_norm]).astype(F32)

    own_gain = attn_norm.astype(F32)[:, None]
    split = lambda weight: (weight.astype(F32) * own_gain).astype(BF).reshape(own_rows, ways, hcols)
    qkv_part = jnp.concatenate(
        [split(query_weight), split(key_weight), split(value_weight)], axis=2
    ).transpose(1, 0, 2)
    qkv_part = lax.all_to_all(qkv_part, "expert", split_axis=0, concat_axis=0, tiled=True)
    w_qkv = lax.all_gather(
        qkv_part.reshape(ways * own_rows, 3 * hcols), "dp", axis=0, tiled=True
    )

    route_cols = routes.astype(BF).reshape(own_rows, -1)
    small = jnp.concatenate([w_router, ffn_norm[:, None], route_cols], axis=1)
    route_end = small.shape[1]
    small = jnp.pad(small, ((0, 0), (0, -route_end % 128)))
    small = lax.all_gather(
        jnp.concatenate([output_weight, small], axis=1), both, axis=0, tiled=True
    )
    w_out, small = small[:, :D], small[:, D:]
    router = small[:, :experts]
    gain_ffn = small[:, experts].astype(F32)[None, :]
    all_routes = lax.dynamic_index_in_dim(
        small[:, experts + 1 : route_end].reshape(dps, ways, own_rows, -1),
        lax.axis_index("dp"),
        0,
        keepdims=False,
    ).reshape(ways, seqs, seg, TOP)
    all_routes = all_routes.transpose(1, 0, 3, 2)

    gate_full = lax.all_gather(w_gate, "dp", axis=1, tiled=True)
    up_full = lax.all_gather(w_up, "dp", axis=1, tiled=True)
    down_full = lax.all_gather(w_down, "dp", axis=1, tiled=True)

    strict = (
        jnp.arange(blk, dtype=jnp.int32)[:, None] < jnp.arange(blk, dtype=jnp.int32)[None, :]
    ).astype(BF)
    slot_ids = jnp.arange(capacity, dtype=jnp.int32)[None, :, None]
    expert_ids = jnp.arange(experts, dtype=jnp.int32)

    def add(total, part):
        return part if total is None else total + part

    def rows_of(array, picks):
        return jnp.concatenate([take_major(array, p) for p in picks], axis=0)

    def attention(s, gathered, *earlier):
        normed = in_order(
            [
                (b * norm_factor(b)).astype(BF)
                for b in (block.astype(F32) for block in gathered)
            ],
            sources,
        )
        qkv = after(dot(normed, w_qkv), *earlier).reshape(ways, SEQ_MB, seg, 3 * hcols)
        mixed, lse = attend(places, qkv, cosine, sine, gains, s.keep)
        vars(s).update(normed=normed, qkv=qkv, lse=lse, mixed_heads=mixed)

    def projection(s):
        mixed = lax.all_to_all(
            s.mixed_heads, "expert", split_axis=0, concat_axis=0, tiled=True
        )
        mixed = mixed.transpose(1, 2, 0, 3).reshape(blk, D)
        hidden = s.rows.astype(F32) + dot(mixed, w_out)
        factor_ffn = norm_factor(hidden)
        routed = (hidden * factor_ffn * gain_ffn).astype(BF)
        vars(s).update(mixed=mixed, hidden=hidden, factor_ffn=factor_ffn, routed=routed)

    def expert_layer(s, routed_all, grad_all, waits):
        routed_blocks = routed_all.reshape(ways, blk, D)
        picked = jnp.stack([take_major(all_routes, p) for p in s.picks], axis=2)
        picked = picked.reshape(ways, TOP, blk).astype(jnp.int32)
        alive = s.live_at.reshape(SEQ_MB, ways, seg).transpose(1, 0, 2).reshape(ways, blk)
        logits = lax.dot_general(
            router, routed_all, (((0,), (1,)), ((), ())), preferred_element_type=F32
        ).reshape(experts, ways, blk)
        chosen = jnp.any(picked[None] == expert_ids[:, None, None, None], axis=2)
        masked = jnp.where(chosen, logits, NEG)
        expo = jnp.exp(masked - jnp.max(masked, axis=0, keepdims=True))
        gates = expo / jnp.sum(expo, axis=0, keepdims=True)
        backs = []
        pin = lambda value, name, j: after(value, *waits.get((name, j), tuple)())
        mixtures = grads_routed = None
        gate_grads = []
        for j in range(local):
            mine = me * local + j
            hits = jnp.any(picked == mine, axis=1) & alive
            rank = dot(hits.astype(BF), strict).astype(jnp.int32)
            select = ((rank[:, None, :] == slot_ids) & hits[:, None, :]).astype(BF)
            gate = take_major(gates, mine)
            slot_gate = jnp.sum(select * gate[:, None, :], axis=2).reshape(slots, 1)
            gather = lambda table: jnp.einsum(
                "bct,btd->bcd", select, table, preferred_element_type=F32
            ).astype(BF).reshape(slots, D)
            combine = lambda made: jnp.einsum(
                "bct,bcd->btd",
                select,
                made.reshape(ways, capacity, D),
                preferred_element_type=F32,
            )
            sent = gather(pin(routed_blocks, "sent", j))
            grad_sent_in = gather(grad_all.reshape(ways, blk, D))
            gate_pre = dot(sent, gate_full[j])
            up_pre = dot(sent, up_full[j])
            sigma = 1.0 / (1.0 + jnp.exp(-gate_pre))
            act = gate_pre * sigma * up_pre
            scaled = (act * slot_gate).astype(BF)
            made = dot(scaled, down_full[j])
            mixtures = add(mixtures, combine(pin(made.astype(BF), "made", j)))
            lifted = dot_nt(grad_sent_in, down_full[j])
            row_dots = jnp.sum(act * lifted, axis=1).reshape(ways, capacity, 1)
            gate_grads.append(jnp.sum(select * row_dots, axis=1))
            grad_act = pin(lifted, "lifted", j) * slot_gate
            grad_up = (grad_act * gate_pre * sigma).astype(BF)
            grad_gate = (grad_act * up_pre * sigma * (1.0 + gate_pre * (1.0 - sigma))).astype(BF)
            grad_in = dot_nt(grad_gate, gate_full[j]) + dot_nt(grad_up, up_full[j])
            grads_routed = add(grads_routed, combine(pin(grad_in.astype(BF), "grad_in", j)))
            backs.append((sent, grad_gate, grad_up, scaled, grad_sent_in))
            s.partial = getattr(s, "partial", grads_routed)
        vars(s).update(
            backs=backs,
            gates=lax.dynamic_index_in_dim(gates, me, 1, keepdims=False),
            gate_grads=jnp.stack(gate_grads, axis=1),
            mixtures=mixtures.astype(BF),
            grads_routed=grads_routed.astype(BF),
        )

    def token_backward(s):
        gate_grad = lax.all_to_all(
            s.gate_grads, "expert", split_axis=0, concat_axis=0, tiled=True
        ).reshape(experts, blk)
        own_gates = s.gates
        grad_logits = own_gates * (
            gate_grad - jnp.sum(own_gates * gate_grad, axis=0, keepdims=True)
        )
        grad_logits = grad_logits.astype(BF)
        grad_routed = s.total_g.astype(F32) + lax.dot_general(
            grad_logits, router, (((0,), (1,)), ((), ())), preferred_element_type=F32
        )
        s.g_router = lax.dot_general(
            s.routed, grad_logits, (((0,), (1,)), ((), ())), preferred_element_type=F32
        )
        hidden, factor_ffn = s.hidden, s.factor_ffn
        s.g_ffn_gain = jnp.sum(grad_routed * hidden * factor_ffn, axis=0, keepdims=True)
        grad_hidden = s.grad_rows.astype(F32) * s.live_col + norm_back(
            grad_routed, hidden, factor_ffn, gain_ffn
        )
        gh = grad_hidden.astype(BF)
        grad_mixed = dot_nt(gh, w_out).astype(BF).reshape(SEQ_MB, seg, ways, hcols)
        grad_mixed = grad_mixed.transpose(2, 0, 1, 3)
        vars(s).update(grad_hidden=grad_hidden, gh=gh, grad_send=grad_mixed)
        s.grad_mixed = lax.all_to_all(
            grad_mixed, "expert", split_axis=0, concat_axis=0, tiled=True
        )

    def attention_backward(s, first, second):
        g_qkv, head_gains = attend_back(
            places, s.qkv, after(s.grad_mixed, *first), s.lse, cosine, sine, gains, s.keep
        )
        s.g_qkv = g_qkv.reshape(ways * blk, 3 * hcols)
        s.g_head_gains = jnp.sum(head_gains, axis=0)
        g_rows = after(s.g_qkv, *second())
        s.parts = dot_nt(g_rows, w_qkv).astype(BF).reshape(ways, blk, D)

    def expert_grad(left, right, *earlier):
        full = jnp.stack(
            [
                sum(
                    dot_tn(after(s.backs[j][left], *earlier), s.backs[j][right])
                    for s in state
                )
                for j in range(local)
            ]
        ).astype(BF)
        return full, lax.psum_scatter(full, "dp", scatter_dimension=1, tiled=True)

    state = []
    for micro in range(MICRO):
        picks = [order[0, micro * SEQ_MB + i] for i in range(SEQ_MB)]
        seq_lens = jnp.stack([lengths[p] for p in picks])
        live_at = positions[None, :] < seq_lens[:, None]
        state.append(
            SimpleNamespace(
                picks=picks,
                live_at=live_at,
                keep=live_at.astype(F32)[:, None, :],
                live_col=lax.dynamic_slice_in_dim(live_at, me * seg, seg, 1)
                .reshape(blk, 1)
                .astype(F32),
                rows=rows_of(tokens, picks),
                grad_rows=rows_of(cotangent, picks),
            )
        )

    one, two = state
    tokens_one = column(one.rows, ways)
    tokens_two = column(two.rows, ways)
    attention(one, tokens_one + partners(tokens_one, ways), tokens_two[1])
    tokens_two = [after(block, one.mixed_heads) for block in tokens_two]
    tokens_two = tokens_two + partners(tokens_two, ways)
    projection(one)
    routed_one = column(after(one.routed, *tokens_two[1 : ways // 2]), ways)
    grads_one = column(one.grad_rows, ways)
    attention(two, [after(block, one.routed) for block in tokens_two], routed_one[1], *grads_one[1:3])
    routed_one = routed_one + partners(routed_one, ways)
    projection(two)
    grads_one = grads_one + partners(grads_one, ways)
    gather_up = lambda value: lax.all_gather(value, "expert", axis=0, tiled=True)
    scatter_sum = lambda value: lax.psum_scatter(
        value.reshape(ways * blk, D), "expert", scatter_dimension=0, tiled=True
    )
    routed_two = gather_up(two.routed)
    grads_two = gather_up(after(two.grad_rows, two.routed))

    expert_layer(
        one,
        after(in_order(routed_one, sources), two.routed),
        in_order(grads_one, sources),
        {},
    )
    one.total_g = scatter_sum(one.grads_routed)
    total_m = scatter_sum(after(one.mixtures, one.total_g))
    one.total_m = lambda: total_m.astype(F32)
    expert_layer(two, after(routed_two, one.mixtures, one.grads_routed), grads_two, {})
    two.total_g = scatter_sum(after(two.grads_routed, total_m))
    one.total_g = after(one.total_g, two.grads_routed)
    token_backward(one)
    full_gate, grad_w_gate = expert_grad(0, 1, one.grad_send)
    full_up, grad_w_up = expert_grad(0, 2, full_gate)
    full_down, grad_w_down = expert_grad(3, 4, full_up)
    two.total_g = after(two.total_g, full_down)
    token_backward(two)
    attention_backward(one, (two.grad_send,), lambda: ())
    one.pair_p = pair_up(one.parts, sources, ways)
    g_out_weight = dot_tn(
        after(jnp.concatenate([s.mixed for s in state], axis=0), one.g_qkv),
        jnp.concatenate([s.gh for s in state], axis=0),
    )
    one.arrived_p = deliver(one.pair_p[1:], ways)
    attention_backward(two, (g_out_weight, one.arrived_p[0]), lambda: ())
    two.pair_p = pair_up(two.parts, sources, ways)
    two.arrived_p = deliver(two.pair_p[1:], ways, *one.arrived_p)
    g_qkv_weight = sum(dot_tn(after(s.normed, *two.pair_p), s.g_qkv) for s in state)
    two.pair_m = pair_up(after(two.mixtures, g_qkv_weight), sources, ways)
    two.total_m = lambda: total_of(two.pair_m[0], deliver(two.pair_m[1:], ways, *two.arrived_p))
    g_router = sum(s.g_router for s in state)
    g_ffn_gain = sum(s.g_ffn_gain for s in state)
    g_head_gains = sum(s.g_head_gains for s in state)

    outputs = jnp.zeros(tokens.shape, BF)
    input_grads = jnp.zeros(tokens.shape, F32)
    for s in state:
        result = (
            (s.hidden + s.total_m()) * s.live_col
        ).astype(BF)
        tokens_f32 = s.rows.astype(F32)
        grad_inputs = s.grad_hidden + norm_back(
            total_of(s.pair_p[0], s.arrived_p), tokens_f32, norm_factor(tokens_f32), 1.0
        )
        for i, p in enumerate(s.picks):
            rows = slice(i * seg, (i + 1) * seg)
            outputs = lax.dynamic_update_index_in_dim(outputs, result[rows], p, 0)
            input_grads = lax.dynamic_update_index_in_dim(input_grads, grad_inputs[rows], p, 0)

    split_own = lambda weight: weight.astype(F32).reshape(own_rows, ways, hcols).transpose(1, 0, 2)
    part = lax.psum_scatter(g_qkv_weight.astype(BF), "dp", scatter_dimension=0, tiled=True)
    part = lax.all_to_all(
        part.reshape(ways, own_rows, 3 * hcols), "expert", split_axis=0, concat_axis=0, tiled=True
    ).astype(F32)
    plain = jnp.sum(
        part[:, :, :hcols] * split_own(query_weight)
        + part[:, :, hcols : 2 * hcols] * split_own(key_weight)
        + part[:, :, 2 * hcols :] * split_own(value_weight),
        axis=(0, 2),
    )
    grad_q, grad_k, grad_v = (
        part[:, :, i * hcols : (i + 1) * hcols].transpose(1, 0, 2).reshape(own_rows, D) * own_gain
        for i in range(3)
    )
    grad_attn_norm = plain
    out_part = lax.psum_scatter(
        g_out_weight.astype(BF), "dp", scatter_dimension=0, tiled=True
    ).reshape(ways, own_rows, D)
    out_pair = pair_up(out_part, sources, ways)
    grad_out = total_of(out_pair[0], deliver(out_pair[1:], ways))

    tiled_gains = jnp.tile(g_head_gains.reshape(2, own_rows, -1), (1, dps * ways, 1))
    small_grads = jnp.concatenate(
        [g_router, g_ffn_gain.T, tiled_gains[0], tiled_gains[1]], axis=1
    )
    small_grads = lax.psum_scatter(small_grads, both, scatter_dimension=0, tiled=True)
    per = HEAD_WIDTH // own_rows
    return (
        outputs,
        input_grads,
        grad_attn_norm,
        grad_q,
        grad_k,
        grad_v,
        small_grads[:, experts + 1 : experts + 1 + per].reshape(HEAD_WIDTH),
        small_grads[:, experts + 1 + per :].reshape(HEAD_WIDTH),
        grad_out,
        small_grads[:, experts],
        small_grads[:, :experts],
        grad_w_gate.astype(F32),
        grad_w_up.astype(F32),
        grad_w_down.astype(F32),
    )


def solution(mesh):
    rows = P(("dp", "expert"), None)
    vector = P(("dp", "expert"))
    seqs = P("dp", "expert", None)
    weights = P("expert", "dp", None)
    return jax.shard_map(
        body,
        mesh=mesh,
        in_specs=(
            seqs,
            seqs,
            P("dp"),
            P("dp", None),
            seqs,
            vector,
            rows,
            rows,
            rows,
            P(),
            P(),
            rows,
            vector,
            rows,
            weights,
            weights,
            weights,
        ),
        out_specs=(
            seqs,
            seqs,
            vector,
            rows,
            rows,
            rows,
            P(),
            P(),
            rows,
            vector,
            rows,
            weights,
            weights,
            weights,
        ),
        check_vma=False,
    )
```

```python
import functools
from types import SimpleNamespace

import jax
import jax.numpy as jnp
from jax import lax
from jax.experimental import pallas as pl
from jax.experimental.pallas import tpu as pltpu
from jax.sharding import PartitionSpec as P

D = 2048
HEAD_COUNT = 16
HEAD_WIDTH = 128
TOP = 8
SEQ_MB = 2
MICRO = 2

EPS = 1e-06
NEG = -1e30
THETA = 10000.0
SCALE = HEAD_WIDTH ** (-0.5)
BF = jnp.bfloat16
F32 = jnp.float32


def dot(a, b):
    return lax.dot_general(a, b, (((1,), (0,)), ((), ())), preferred_element_type=F32)


def dot_nt(a, b):
    return lax.dot_general(a, b, (((1,), (1,)), ((), ())), preferred_element_type=F32)


def dot_tn(a, b):
    return lax.dot_general(a, b, (((0,), (0,)), ((), ())), preferred_element_type=F32)


def norm_factor(values):
    return lax.rsqrt(jnp.mean(values * values, axis=-1, keepdims=True) + EPS)


def norm_back(grad_after, rows, factor, gain):
    scaled = grad_after * gain
    shift = jnp.mean(scaled * rows, axis=-1, keepdims=True)
    return factor * scaled - rows * (factor * factor * factor * shift)


def swap_halves(values):
    return pltpu.roll(values, HEAD_WIDTH // 2, 1)


def head_columns(ref, index, length):
    cols = ref[:, 0, :, index * HEAD_WIDTH : (index + 1) * HEAD_WIDTH]
    return cols.reshape(length, HEAD_WIDTH)


def rotated(rows, gain, cosine, sine):
    factor = norm_factor(rows)
    normed = rows * factor * gain
    return (normed * cosine + swap_halves(normed) * sine).astype(BF), factor


def attend_kernel(
    place_ref, qkv_ref, cos_ref, sin_ref, gains_ref, keep_ref, mixed_ref, lse_ref, *, heads, tile
):
    blocks, _, seg, _ = qkv_ref.shape
    length = blocks * seg
    cosine = cos_ref[...]
    sine = sin_ref[...]
    keep = keep_ref[0] > 0
    for head in range(heads):
        q_rot, _ = rotated(head_columns(qkv_ref, head, length), gains_ref[0:1], cosine, sine)
        k_rot, _ = rotated(
            head_columns(qkv_ref, heads + head, length), gains_ref[1:2], cosine, sine
        )
        values = head_columns(qkv_ref, 2 * heads + head, length).astype(BF)
        for step in range(length // tile):
            rows = slice(step * tile, (step + 1) * tile)
            scores = jnp.where(keep, dot_nt(q_rot[rows], k_rot) * SCALE, NEG)
            peak = jnp.max(scores, axis=-1, keepdims=True)
            expo = jnp.exp(scores - peak)
            total = jnp.sum(expo, axis=-1, keepdims=True)
            mixed = dot((expo * (1.0 / total)).astype(BF), values)
            mixed = mixed.astype(BF)
            for sub in range(tile // seg):
                mixed_ref[
                    place_ref[step * tile // seg + sub],
                    0,
                    :,
                    head * HEAD_WIDTH : (head + 1) * HEAD_WIDTH,
                ] = mixed[sub * seg : (sub + 1) * seg]
            lse_ref[0, head, rows, :] = jnp.broadcast_to(
                peak + jnp.log(total), (tile, HEAD_WIDTH)
            )


def attend_back_kernel(
    place_ref,
    qkv_ref,
    grad_ref,
    lse_ref,
    cos_ref,
    sin_ref,
    gains_ref,
    keep_ref,
    out_ref,
    gain_ref,
    dq_ref,
    dk_ref,
    dv_ref,
    *,
    heads,
    tile,
):
    blocks, _, seg, _ = qkv_ref.shape
    length = blocks * seg
    cosine = cos_ref[...]
    sine = sin_ref[...]
    keep = keep_ref[0] > 0
    gain_sums = [jnp.zeros((1, HEAD_WIDTH), F32), jnp.zeros((1, HEAD_WIDTH), F32)]

    def store(index, rows):
        out_ref[:, 0, :, index * HEAD_WIDTH : (index + 1) * HEAD_WIDTH] = rows.astype(BF).reshape(
            blocks, seg, HEAD_WIDTH
        )

    for head in range(heads):
        q_rows = head_columns(qkv_ref, head, length)
        k_rows = head_columns(qkv_ref, heads + head, length)
        q_rot, q_factor = rotated(q_rows, gains_ref[0:1], cosine, sine)
        k_rot, k_factor = rotated(k_rows, gains_ref[1:2], cosine, sine)
        values = head_columns(qkv_ref, 2 * heads + head, length).astype(BF)
        grads = jnp.concatenate(
            [
                grad_ref[place_ref[b], 0, :, head * HEAD_WIDTH : (head + 1) * HEAD_WIDTH]
                for b in range(blocks)
            ],
            axis=0,
        )
        for step in range(length // tile):
            rows = slice(step * tile, (step + 1) * tile)
            scores = jnp.where(keep, dot_nt(q_rot[rows], k_rot) * SCALE, NEG)
            probs = jnp.exp(scores - lse_ref[0, head, rows, 0:1])
            grad_probs = dot_nt(grads[rows], values)
            inner = jnp.sum(probs * grad_probs, axis=-1, keepdims=True)
            grad_scores = (probs * (grad_probs - inner)).astype(BF)
            dq_ref[rows, :] = dot(grad_scores, k_rot) * SCALE
            dk = dot_tn(grad_scores, q_rot[rows])
            dv = dot_tn(probs.astype(BF), grads[rows])
            if step == 0:
                dk_ref[...] = dk
                dv_ref[...] = dv
            else:
                dk_ref[...] += dk
                dv_ref[...] += dv
        for which, (acc_ref, factor, source, scale) in enumerate(
            ((dq_ref, q_factor, q_rows, 1.0), (dk_ref, k_factor, k_rows, SCALE))
        ):
            grad = acc_ref[...] * scale
            grad = grad * cosine - swap_halves(grad) * sine
            gain_sums[which] += jnp.sum(grad * source * factor, axis=0, keepdims=True)
            store(
                which * heads + head,
                norm_back(grad, source, factor, gains_ref[which : which + 1]),
            )
        store(2 * heads + head, dv_ref[...])
    gain_ref[0] = jnp.concatenate(gain_sums, axis=0)


def attend(places, qkv, cosine, sine, gains, keep):
    blocks, seqs, seg, width = qkv.shape
    length = blocks * seg
    heads = width // (3 * HEAD_WIDTH)
    tile = max(length // 4, seg)
    full = lambda shape: pl.BlockSpec(shape, lambda s: (0,) * len(shape))
    return pl.pallas_call(
        functools.partial(attend_kernel, heads=heads, tile=tile),
        grid=(seqs,),
        in_specs=[
            pl.BlockSpec(memory_space=pltpu.SMEM),
            pl.BlockSpec((blocks, 1, seg, width), lambda s: (0, s, 0, 0)),
            full((length, HEAD_WIDTH)),
            full((length, HEAD_WIDTH)),
            full((2, HEAD_WIDTH)),
            pl.BlockSpec((1, 1, length), lambda s: (s, 0, 0)),
        ],
        out_specs=[
            pl.BlockSpec((blocks, 1, seg, heads * HEAD_WIDTH), lambda s: (0, s, 0, 0)),
            pl.BlockSpec((1, heads, length, HEAD_WIDTH), lambda s: (s, 0, 0, 0)),
        ],
        out_shape=[
            jax.ShapeDtypeStruct((blocks, seqs, seg, heads * HEAD_WIDTH), BF),
            jax.ShapeDtypeStruct((seqs, heads, length, HEAD_WIDTH), F32),
        ],
        name="attend",
    )(places, qkv, cosine, sine, gains, keep)


def attend_back(places, qkv, grads, lse, cosine, sine, gains, keep):
    blocks, seqs, seg, width = qkv.shape
    length = blocks * seg
    heads = width // (3 * HEAD_WIDTH)
    tile = max(length // 4, seg)
    full = lambda shape: pl.BlockSpec(shape, lambda s: (0,) * len(shape))
    return pl.pallas_call(
        functools.partial(attend_back_kernel, heads=heads, tile=tile),
        grid=(seqs,),
        in_specs=[
            pl.BlockSpec(memory_space=pltpu.SMEM),
            pl.BlockSpec((blocks, 1, seg, width), lambda s: (0, s, 0, 0)),
            pl.BlockSpec((blocks, 1, seg, heads * HEAD_WIDTH), lambda s: (0, s, 0, 0)),
            pl.BlockSpec((1, heads, length, HEAD_WIDTH), lambda s: (s, 0, 0, 0)),
            full((length, HEAD_WIDTH)),
            full((length, HEAD_WIDTH)),
            full((2, HEAD_WIDTH)),
            pl.BlockSpec((1, 1, length), lambda s: (s, 0, 0)),
        ],
        out_specs=[
            pl.BlockSpec((blocks, 1, seg, width), lambda s: (0, s, 0, 0)),
            pl.BlockSpec((1, 2, HEAD_WIDTH), lambda s: (s, 0, 0)),
        ],
        out_shape=[
            jax.ShapeDtypeStruct((blocks, seqs, seg, width), BF),
            jax.ShapeDtypeStruct((seqs, 2, HEAD_WIDTH), F32),
        ],
        scratch_shapes=[pltpu.VMEM((length, HEAD_WIDTH), F32)] * 3,
        name="attend_back",
    )(places, qkv, grads, lse, cosine, sine, gains, keep)


def rotate(value, ways, move):
    chips = ways // 2
    pairs = [(2 * s + k, 2 * ((s + move) % chips) + k) for s in range(chips) for k in (0, 1)]
    return lax.ppermute(value, "expert", pairs)


def exchange(value, ways):
    return lax.ppermute(value, "expert", [(e, e ^ 1) for e in range(ways)])


def column(block, ways):
    return [block] + [rotate(block, ways, h) for h in range(1, ways // 2)]


def partners(blocks, ways):
    return [exchange(value, ways) for value in blocks]


def pair_up(parts, sources, ways):
    chips = ways // 2
    mine = [take_major(parts, sources[h]) for h in range(chips)]
    other = exchange(jnp.stack([take_major(parts, sources[chips + h]) for h in range(chips)]), ways)
    own = mine[0].astype(F32) + other[0].astype(F32)
    rest = [(mine[h].astype(F32) + other[h].astype(F32)).astype(BF) for h in range(1, chips)]
    return lax.optimization_barrier((own, *rest))


def in_order(blocks, sources):
    whole = jnp.zeros((len(blocks),) + blocks[0].shape, blocks[0].dtype)
    for place, block in enumerate(blocks):
        whole = lax.dynamic_update_index_in_dim(whole, block, sources[place], 0)
    return whole.reshape((-1,) + blocks[0].shape[1:])


def deliver(rest, ways, *earlier):
    return [rotate(after(part, *earlier), ways, -(h + 1)) for h, part in enumerate(rest)]


def total_of(own, arrived):
    for part in arrived:
        own = own + part.astype(F32)
    return own


def after(value, *earlier):
    return lax.optimization_barrier((value,) + earlier)[0]


def take_major(array, index):
    return lax.dynamic_index_in_dim(array, index, 0, keepdims=False)


def body(
    tokens,
    cotangent,
    lengths,
    order,
    routes,
    attn_norm,
    query_weight,
    key_weight,
    value_weight,
    q_norm,
    k_norm,
    output_weight,
    ffn_norm,
    w_router,
    w_gate,
    w_up,
    w_down,
):
    both = ("dp", "expert")
    dps = lax.axis_size("dp")
    ways = lax.axis_size("expert")
    chips = ways // 2
    me = lax.axis_index("expert")
    chip, core = me // 2, me % 2
    seqs, seg, _ = tokens.shape
    length = seg * ways
    blk = SEQ_MB * seg
    own_rows = attn_norm.shape[0]
    experts = w_router.shape[1]
    capacity = blk * TOP // experts
    local = w_gate.shape[0]
    ff = w_gate.shape[2]
    hcols = D // ways
    slots = ways * capacity

    sources = jnp.stack(
        [((chip + chips - h) % chips) * 2 + (core ^ cc) for cc in (0, 1) for h in range(chips)]
    )
    positions = jnp.arange(length, dtype=jnp.int32)
    places = jnp.arange(ways, dtype=jnp.int32)
    inverse = THETA ** (-(2.0 * jnp.arange(HEAD_WIDTH // 2, dtype=F32)) / HEAD_WIDTH)
    angles = positions.astype(F32)[:, None] * inverse[None, :]
    cosine = jnp.concatenate([jnp.cos(angles)] * 2, axis=1)
    sine = jnp.concatenate([-jnp.sin(angles), jnp.sin(angles)], axis=1)
    gains = jnp.stack([q_norm, k_norm]).astype(F32)

    own_gain = attn_norm.astype(F32)[:, None]
    split = lambda weight: (weight.astype(F32) * own_gain).astype(BF).reshape(own_rows, ways, hcols)
    qkv_part = jnp.concatenate(
        [split(query_weight), split(key_weight), split(value_weight)], axis=2
    ).transpose(1, 0, 2)
    qkv_part = lax.all_to_all(qkv_part, "expert", split_axis=0, concat_axis=0, tiled=True)
    w_qkv = lax.all_gather(
        qkv_part.reshape(ways * own_rows, 3 * hcols), "dp", axis=0, tiled=True
    )

    route_cols = routes.astype(BF).reshape(own_rows, -1)
    small = jnp.concatenate([w_router, ffn_norm[:, None], route_cols], axis=1)
    route_end = small.shape[1]
    small = jnp.pad(small, ((0, 0), (0, -route_end % 128)))
    small = lax.all_gather(
        jnp.concatenate([output_weight, small], axis=1), both, axis=0, tiled=True
    )
    w_out, small = small[:, :D], small[:, D:]
    router = small[:, :experts]
    gain_ffn = small[:, experts].astype(F32)[None, :]
    all_routes = lax.dynamic_index_in_dim(
        small[:, experts + 1 : route_end].reshape(dps, ways, own_rows, -1),
        lax.axis_index("dp"),
        0,
        keepdims=False,
    ).reshape(ways, seqs, seg, TOP)
    all_routes = all_routes.transpose(1, 0, 3, 2)

    gate_full = lax.all_gather(w_gate, "dp", axis=1, tiled=True)
    up_full = lax.all_gather(w_up, "dp", axis=1, tiled=True)
    down_full = lax.all_gather(w_down, "dp", axis=1, tiled=True)

    strict = (
        jnp.arange(blk, dtype=jnp.int32)[:, None] < jnp.arange(blk, dtype=jnp.int32)[None, :]
    ).astype(BF)
    slot_ids = jnp.arange(capacity, dtype=jnp.int32)[None, :, None]
    expert_ids = jnp.arange(experts, dtype=jnp.int32)

    def add(total, part):
        return part if total is None else total + part

    def rows_of(array, picks):
        return jnp.concatenate([take_major(array, p) for p in picks], axis=0)

    def attention(s, gathered, *earlier):
        normed = in_order(
            [
                (b * norm_factor(b)).astype(BF)
                for b in (block.astype(F32) for block in gathered)
            ],
            sources,
        )
        qkv = after(dot(normed, w_qkv), *earlier).reshape(ways, SEQ_MB, seg, 3 * hcols)
        mixed, lse = attend(places, qkv, cosine, sine, gains, s.keep)
        vars(s).update(normed=normed, qkv=qkv, lse=lse, mixed_heads=mixed)

    def projection(s, *earlier):
        mixed = lax.all_to_all(
            s.mixed_heads, "expert", split_axis=0, concat_axis=0, tiled=True
        )
        mixed = after(mixed, *earlier).transpose(1, 2, 0, 3).reshape(blk, D)
        hidden = s.rows.astype(F32) + dot(mixed, w_out)
        factor_ffn = norm_factor(hidden)
        routed = (hidden * factor_ffn * gain_ffn).astype(BF)
        vars(s).update(mixed=mixed, hidden=hidden, factor_ffn=factor_ffn, routed=routed)

    def expert_layer(s, routed_all, grad_all, waits):
        routed_blocks = routed_all.reshape(ways, blk, D)
        picked = jnp.stack([take_major(all_routes, p) for p in s.picks], axis=2)
        picked = picked.reshape(ways, TOP, blk).astype(jnp.int32)
        alive = s.live_at.reshape(SEQ_MB, ways, seg).transpose(1, 0, 2).reshape(ways, blk)
        logits = lax.dot_general(
            router, routed_all, (((0,), (1,)), ((), ())), preferred_element_type=F32
        ).reshape(experts, ways, blk)
        chosen = jnp.any(picked[None] == expert_ids[:, None, None, None], axis=2)
        masked = jnp.where(chosen, logits, NEG)
        expo = jnp.exp(masked - jnp.max(masked, axis=0, keepdims=True))
        gates = expo / jnp.sum(expo, axis=0, keepdims=True)
        backs = []
        pin = lambda value, name, j: after(value, *waits.get((name, j), tuple)())
        mixtures = grads_routed = None
        gate_grads = []
        for j in range(local):
            mine = me * local + j
            hits = jnp.any(picked == mine, axis=1) & alive
            rank = dot(hits.astype(BF), strict).astype(jnp.int32)
            select = ((rank[:, None, :] == slot_ids) & hits[:, None, :]).astype(BF)
            gate = take_major(gates, mine)
            slot_gate = jnp.sum(select * gate[:, None, :], axis=2).reshape(slots, 1)
            gather = lambda table: jnp.einsum(
                "bct,btd->bcd", select, table, preferred_element_type=F32
            ).astype(BF).reshape(slots, D)
            combine = lambda made: jnp.einsum(
                "bct,bcd->btd",
                select,
                made.reshape(ways, capacity, D),
                preferred_element_type=F32,
            )
            sent = gather(pin(routed_blocks, "sent", j))
            grad_sent_in = gather(grad_all.reshape(ways, blk, D))
            gate_pre = dot(sent, gate_full[j])
            up_pre = dot(sent, up_full[j])
            sigma = 1.0 / (1.0 + jnp.exp(-gate_pre))
            act = gate_pre * sigma * up_pre
            scaled = (act * slot_gate).astype(BF)
            made = dot(scaled, down_full[j])
            mixtures = add(mixtures, combine(pin(made.astype(BF), "made", j)))
            lifted = dot_nt(grad_sent_in, down_full[j])
            row_dots = jnp.sum(act * lifted, axis=1).reshape(ways, capacity, 1)
            gate_grads.append(jnp.sum(select * row_dots, axis=1))
            grad_act = pin(lifted, "lifted", j) * slot_gate
            grad_up = (grad_act * gate_pre * sigma).astype(BF)
            grad_gate = (grad_act * up_pre * sigma * (1.0 + gate_pre * (1.0 - sigma))).astype(BF)
            grad_in = dot_nt(grad_gate, gate_full[j]) + dot_nt(grad_up, up_full[j])
            grads_routed = add(grads_routed, combine(pin(grad_in.astype(BF), "grad_in", j)))
            backs.append((sent, grad_gate, grad_up, scaled, grad_sent_in))
            s.partial = getattr(s, "partial", grads_routed)
        vars(s).update(
            backs=backs,
            gates=lax.dynamic_index_in_dim(gates, me, 1, keepdims=False),
            gate_grads=jnp.stack(gate_grads, axis=1),
            mixtures=mixtures.astype(BF),
            grads_routed=grads_routed.astype(BF),
        )

    def token_backward(s):
        gate_grad = lax.all_to_all(
            s.gate_grads, "expert", split_axis=0, concat_axis=0, tiled=True
        ).reshape(experts, blk)
        own_gates = s.gates
        grad_logits = own_gates * (
            gate_grad - jnp.sum(own_gates * gate_grad, axis=0, keepdims=True)
        )
        grad_logits = grad_logits.astype(BF)
        grad_routed = s.total_g.astype(F32) + lax.dot_general(
            grad_logits, router, (((0,), (1,)), ((), ())), preferred_element_type=F32
        )
        s.g_router = lax.dot_general(
            s.routed, grad_logits, (((0,), (1,)), ((), ())), preferred_element_type=F32
        )
        hidden, factor_ffn = s.hidden, s.factor_ffn
        s.g_ffn_gain = jnp.sum(grad_routed * hidden * factor_ffn, axis=0, keepdims=True)
        grad_hidden = s.grad_rows.astype(F32) * s.live_col + norm_back(
            grad_routed, hidden, factor_ffn, gain_ffn
        )
        gh = grad_hidden.astype(BF)
        grad_mixed = dot_nt(gh, w_out).astype(BF).reshape(SEQ_MB, seg, ways, hcols)
        grad_mixed = grad_mixed.transpose(2, 0, 1, 3)
        vars(s).update(grad_hidden=grad_hidden, gh=gh, grad_send=grad_mixed)
        s.grad_mixed = lax.all_to_all(
            grad_mixed, "expert", split_axis=0, concat_axis=0, tiled=True
        )

    def attention_backward(s, first, second):
        g_qkv, head_gains = attend_back(
            places, s.qkv, after(s.grad_mixed, *first), s.lse, cosine, sine, gains, s.keep
        )
        s.g_qkv = g_qkv.reshape(ways * blk, 3 * hcols)
        s.g_head_gains = jnp.sum(head_gains, axis=0)
        g_rows = after(s.g_qkv, *second())
        s.parts = dot_nt(g_rows, w_qkv).astype(BF).reshape(ways, blk, D)

    def expert_grad(left, right, *earlier):
        full = jnp.stack(
            [
                sum(
                    dot_tn(after(s.backs[j][left], *earlier), s.backs[j][right])
                    for s in state
                )
                for j in range(local)
            ]
        ).astype(BF)
        return full, lax.psum_scatter(full, "dp", scatter_dimension=1, tiled=True)

    state = []
    for micro in range(MICRO):
        picks = [order[0, micro * SEQ_MB + i] for i in range(SEQ_MB)]
        seq_lens = jnp.stack([lengths[p] for p in picks])
        live_at = positions[None, :] < seq_lens[:, None]
        state.append(
            SimpleNamespace(
                picks=picks,
                live_at=live_at,
                keep=live_at.astype(F32)[:, None, :],
                live_col=lax.dynamic_slice_in_dim(live_at, me * seg, seg, 1)
                .reshape(blk, 1)
                .astype(F32),
                rows=rows_of(tokens, picks),
                grad_rows=rows_of(cotangent, picks),
            )
        )

    one, two = state
    tokens_one = column(one.rows, ways)
    tokens_two = column(two.rows, ways)
    grads_one = column(one.grad_rows, ways)
    attention(
        one,
        [after(block, *tokens_two[1:]) for block in tokens_one + partners(tokens_one, ways)],
        grads_one[1],
    )
    tokens_two = [after(block, one.mixed_heads, grads_one[2]) for block in tokens_two]
    projection(one)
    routed_one = column(one.routed, ways)
    attention(two, tokens_two + partners(tokens_two, ways), one.routed, *grads_one[3:])
    routed_one = routed_one + partners(routed_one, ways)
    projection(two, *routed_one[1 : ways // 2])
    grads_one = grads_one + partners(grads_one, ways)
    gather_up = lambda value: lax.all_gather(value, "expert", axis=0, tiled=True)
    scatter_sum = lambda value: lax.psum_scatter(
        value.reshape(ways * blk, D), "expert", scatter_dimension=0, tiled=True
    )
    routed_two = gather_up(two.routed)
    grads_two = gather_up(after(two.grad_rows, two.routed))

    expert_layer(
        one,
        after(in_order(routed_one, sources), two.routed),
        in_order(grads_one, sources),
        {},
    )
    one.total_g = scatter_sum(one.grads_routed)
    total_m = scatter_sum(after(one.mixtures, one.total_g))
    one.total_m = lambda: total_m.astype(F32)
    expert_layer(two, after(routed_two, one.mixtures, one.grads_routed), grads_two, {})
    two.total_g = scatter_sum(after(two.grads_routed, total_m))
    one.total_g = after(one.total_g, two.grads_routed)
    token_backward(one)
    full_gate, grad_w_gate = expert_grad(0, 1, one.grad_send)
    full_up, grad_w_up = expert_grad(0, 2, full_gate)
    full_down, grad_w_down = expert_grad(3, 4, full_up)
    two.total_g = after(two.total_g, full_down)
    token_backward(two)
    two.pair_m = pair_up(two.mixtures, sources, ways)
    two.arrived_m = deliver(two.pair_m[1:], ways)
    attention_backward(one, (two.grad_send, two.arrived_m[0]), lambda: (two.arrived_m[1],))
    one.pair_p = pair_up(one.parts, sources, ways)
    g_out_weight = dot_tn(
        after(jnp.concatenate([s.mixed for s in state], axis=0), one.g_qkv)
        .reshape(-1, dps, 2, D // dps // 2)
        .transpose(0, 2, 1, 3)
        .reshape(-1, D),
        jnp.concatenate([s.gh for s in state], axis=0),
    ).reshape(2, D // 2, D)
    one.arrived_p = deliver(one.pair_p[1:], ways)
    attention_backward(
        two, (g_out_weight, two.arrived_m[-1], one.arrived_p[0]), lambda: (one.arrived_p[1],)
    )
    two.pair_p = pair_up(two.parts, sources, ways)
    two.arrived_p = deliver(two.pair_p[1:], ways, *one.arrived_p)
    g_qkv_weight = sum(
        dot_tn(after(s.normed, one.arrived_p[-1], *two.pair_p), s.g_qkv) for s in state
    )
    two.total_m = lambda: total_of(two.pair_m[0], two.arrived_m)
    g_router = sum(s.g_router for s in state)
    g_ffn_gain = sum(s.g_ffn_gain for s in state)
    g_head_gains = sum(s.g_head_gains for s in state)

    outputs = jnp.zeros(tokens.shape, BF)
    input_grads = jnp.zeros(tokens.shape, F32)
    for s in state:
        result = (
            (s.hidden + s.total_m()) * s.live_col
        ).astype(BF)
        tokens_f32 = s.rows.astype(F32)
        grad_inputs = s.grad_hidden + norm_back(
            total_of(s.pair_p[0], s.arrived_p), tokens_f32, norm_factor(tokens_f32), 1.0
        )
        for i, p in enumerate(s.picks):
            rows = slice(i * seg, (i + 1) * seg)
            outputs = lax.dynamic_update_index_in_dim(outputs, result[rows], p, 0)
            input_grads = lax.dynamic_update_index_in_dim(input_grads, grad_inputs[rows], p, 0)

    split_own = lambda weight: weight.astype(F32).reshape(own_rows, ways, hcols).transpose(1, 0, 2)
    part = lax.psum_scatter(g_qkv_weight.astype(BF), "dp", scatter_dimension=0, tiled=True)
    part = lax.all_to_all(
        part.reshape(ways, own_rows, 3 * hcols), "expert", split_axis=0, concat_axis=0, tiled=True
    ).astype(F32)
    plain = jnp.sum(
        part[:, :, :hcols] * split_own(query_weight)
        + part[:, :, hcols : 2 * hcols] * split_own(key_weight)
        + part[:, :, 2 * hcols :] * split_own(value_weight),
        axis=(0, 2),
    )
    grad_q, grad_k, grad_v = (
        part[:, :, i * hcols : (i + 1) * hcols].transpose(1, 0, 2).reshape(own_rows, D) * own_gain
        for i in range(3)
    )
    grad_attn_norm = plain
    out_part = lax.psum_scatter(
        g_out_weight.astype(BF), "dp", scatter_dimension=1, tiled=True
    ).reshape(ways, own_rows, D)
    out_pair = pair_up(out_part, sources, ways)
    grad_out = total_of(out_pair[0], deliver(out_pair[1:], ways))

    tiled_gains = jnp.tile(g_head_gains.reshape(2, own_rows, -1), (1, dps * ways, 1))
    small_grads = jnp.concatenate(
        [g_router, g_ffn_gain.T, tiled_gains[0], tiled_gains[1]], axis=1
    )
    small_grads = small_grads.reshape(dps, ways, own_rows, -1)
    small_grads = jnp.sum(
        lax.all_to_all(small_grads, "expert", split_axis=1, concat_axis=1, tiled=True), axis=1
    )
    small_grads = jnp.sum(
        lax.all_to_all(small_grads, "dp", split_axis=0, concat_axis=0, tiled=True), axis=0
    )
    per = HEAD_WIDTH // own_rows
    return (
        outputs,
        input_grads,
        grad_attn_norm,
        grad_q,
        grad_k,
        grad_v,
        small_grads[:, experts + 1 : experts + 1 + per].reshape(HEAD_WIDTH),
        small_grads[:, experts + 1 + per :].reshape(HEAD_WIDTH),
        grad_out,
        small_grads[:, experts],
        small_grads[:, :experts],
        grad_w_gate.astype(F32),
        grad_w_up.astype(F32),
        grad_w_down.astype(F32),
    )


def solution(mesh):
    rows = P(("dp", "expert"), None)
    vector = P(("dp", "expert"))
    seqs = P("dp", "expert", None)
    weights = P("expert", "dp", None)
    return jax.shard_map(
        body,
        mesh=mesh,
        in_specs=(
            seqs,
            seqs,
            P("dp"),
            P("dp", None),
            seqs,
            vector,
            rows,
            rows,
            rows,
            P(),
            P(),
            rows,
            vector,
            rows,
            weights,
            weights,
            weights,
        ),
        out_specs=(
            seqs,
            seqs,
            vector,
            rows,
            rows,
            rows,
            P(),
            P(),
            rows,
            vector,
            rows,
            weights,
            weights,
            weights,
        ),
        check_vma=False,
    )
```

```python
import functools
from types import SimpleNamespace

import jax
import jax.numpy as jnp
from jax import lax
from jax.experimental import pallas as pl
from jax.experimental.pallas import tpu as pltpu
from jax.sharding import PartitionSpec as P

D = 2048
HEAD_COUNT = 16
HEAD_WIDTH = 128
TOP = 8
SEQ_MB = 2
MICRO = 2

EPS = 1e-06
NEG = -1e30
THETA = 10000.0
SCALE = HEAD_WIDTH ** (-0.5)
BF = jnp.bfloat16
F32 = jnp.float32


def dot(a, b):
    return lax.dot_general(a, b, (((1,), (0,)), ((), ())), preferred_element_type=F32)


def dot_nt(a, b):
    return lax.dot_general(a, b, (((1,), (1,)), ((), ())), preferred_element_type=F32)


def dot_tn(a, b):
    return lax.dot_general(a, b, (((0,), (0,)), ((), ())), preferred_element_type=F32)


def norm_factor(values):
    return lax.rsqrt(jnp.mean(values * values, axis=-1, keepdims=True) + EPS)


def norm_back(grad_after, rows, factor, gain):
    scaled = grad_after * gain
    shift = jnp.mean(scaled * rows, axis=-1, keepdims=True)
    return factor * scaled - rows * (factor * factor * factor * shift)


def swap_halves(values):
    return pltpu.roll(values, HEAD_WIDTH // 2, 1)


def head_columns(ref, index, length):
    cols = ref[:, 0, :, index * HEAD_WIDTH : (index + 1) * HEAD_WIDTH]
    return cols.reshape(length, HEAD_WIDTH)


def rotated(rows, gain, cosine, sine):
    factor = norm_factor(rows)
    normed = rows * factor * gain
    return (normed * cosine + swap_halves(normed) * sine).astype(BF), factor


def attend_kernel(
    place_ref, qkv_ref, cos_ref, sin_ref, gains_ref, keep_ref, mixed_ref, lse_ref, *, heads, tile
):
    blocks, _, seg, _ = qkv_ref.shape
    length = blocks * seg
    cosine = cos_ref[...]
    sine = sin_ref[...]
    keep = keep_ref[0] > 0
    for head in range(heads):
        q_rot, _ = rotated(head_columns(qkv_ref, head, length), gains_ref[0:1], cosine, sine)
        k_rot, _ = rotated(
            head_columns(qkv_ref, heads + head, length), gains_ref[1:2], cosine, sine
        )
        values = head_columns(qkv_ref, 2 * heads + head, length).astype(BF)
        for step in range(length // tile):
            rows = slice(step * tile, (step + 1) * tile)
            scores = jnp.where(keep, dot_nt(q_rot[rows], k_rot) * SCALE, NEG)
            peak = jnp.max(scores, axis=-1, keepdims=True)
            expo = jnp.exp(scores - peak)
            total = jnp.sum(expo, axis=-1, keepdims=True)
            mixed = dot((expo * (1.0 / total)).astype(BF), values)
            mixed = mixed.astype(BF)
            for sub in range(tile // seg):
                mixed_ref[
                    place_ref[step * tile // seg + sub],
                    0,
                    :,
                    head * HEAD_WIDTH : (head + 1) * HEAD_WIDTH,
                ] = mixed[sub * seg : (sub + 1) * seg]
            lse_ref[0, head, rows, :] = jnp.broadcast_to(
                peak + jnp.log(total), (tile, HEAD_WIDTH)
            )


def attend_back_kernel(
    place_ref,
    qkv_ref,
    grad_ref,
    lse_ref,
    cos_ref,
    sin_ref,
    gains_ref,
    keep_ref,
    out_ref,
    gain_ref,
    dq_ref,
    dk_ref,
    dv_ref,
    *,
    heads,
    tile,
):
    blocks, _, seg, _ = qkv_ref.shape
    length = blocks * seg
    cosine = cos_ref[...]
    sine = sin_ref[...]
    keep = keep_ref[0] > 0
    gain_sums = [jnp.zeros((1, HEAD_WIDTH), F32), jnp.zeros((1, HEAD_WIDTH), F32)]

    def store(index, rows):
        out_ref[:, 0, :, index * HEAD_WIDTH : (index + 1) * HEAD_WIDTH] = rows.astype(BF).reshape(
            blocks, seg, HEAD_WIDTH
        )

    for head in range(heads):
        q_rows = head_columns(qkv_ref, head, length)
        k_rows = head_columns(qkv_ref, heads + head, length)
        q_rot, q_factor = rotated(q_rows, gains_ref[0:1], cosine, sine)
        k_rot, k_factor = rotated(k_rows, gains_ref[1:2], cosine, sine)
        values = head_columns(qkv_ref, 2 * heads + head, length).astype(BF)
        grads = jnp.concatenate(
            [
                grad_ref[place_ref[b], 0, :, head * HEAD_WIDTH : (head + 1) * HEAD_WIDTH]
                for b in range(blocks)
            ],
            axis=0,
        )
        for step in range(length // tile):
            rows = slice(step * tile, (step + 1) * tile)
            scores = jnp.where(keep, dot_nt(q_rot[rows], k_rot) * SCALE, NEG)
            probs = jnp.exp(scores - lse_ref[0, head, rows, 0:1])
            grad_probs = dot_nt(grads[rows], values)
            inner = jnp.sum(probs * grad_probs, axis=-1, keepdims=True)
            grad_scores = (probs * (grad_probs - inner)).astype(BF)
            dq_ref[rows, :] = dot(grad_scores, k_rot) * SCALE
            dk = dot_tn(grad_scores, q_rot[rows])
            dv = dot_tn(probs.astype(BF), grads[rows])
            if step == 0:
                dk_ref[...] = dk
                dv_ref[...] = dv
            else:
                dk_ref[...] += dk
                dv_ref[...] += dv
        for which, (acc_ref, factor, source, scale) in enumerate(
            ((dq_ref, q_factor, q_rows, 1.0), (dk_ref, k_factor, k_rows, SCALE))
        ):
            grad = acc_ref[...] * scale
            grad = grad * cosine - swap_halves(grad) * sine
            gain_sums[which] += jnp.sum(grad * source * factor, axis=0, keepdims=True)
            store(
                which * heads + head,
                norm_back(grad, source, factor, gains_ref[which : which + 1]),
            )
        store(2 * heads + head, dv_ref[...])
    gain_ref[0] = jnp.concatenate(gain_sums, axis=0)


def attend(places, qkv, cosine, sine, gains, keep):
    blocks, seqs, seg, width = qkv.shape
    length = blocks * seg
    heads = width // (3 * HEAD_WIDTH)
    tile = max(length // 4, seg)
    full = lambda shape: pl.BlockSpec(shape, lambda s: (0,) * len(shape))
    return pl.pallas_call(
        functools.partial(attend_kernel, heads=heads, tile=tile),
        grid=(seqs,),
        in_specs=[
            pl.BlockSpec(memory_space=pltpu.SMEM),
            pl.BlockSpec((blocks, 1, seg, width), lambda s: (0, s, 0, 0)),
            full((length, HEAD_WIDTH)),
            full((length, HEAD_WIDTH)),
            full((2, HEAD_WIDTH)),
            pl.BlockSpec((1, 1, length), lambda s: (s, 0, 0)),
        ],
        out_specs=[
            pl.BlockSpec((blocks, 1, seg, heads * HEAD_WIDTH), lambda s: (0, s, 0, 0)),
            pl.BlockSpec((1, heads, length, HEAD_WIDTH), lambda s: (s, 0, 0, 0)),
        ],
        out_shape=[
            jax.ShapeDtypeStruct((blocks, seqs, seg, heads * HEAD_WIDTH), BF),
            jax.ShapeDtypeStruct((seqs, heads, length, HEAD_WIDTH), F32),
        ],
        name="attend",
    )(places, qkv, cosine, sine, gains, keep)


def attend_back(places, qkv, grads, lse, cosine, sine, gains, keep):
    blocks, seqs, seg, width = qkv.shape
    length = blocks * seg
    heads = width // (3 * HEAD_WIDTH)
    tile = max(length // 4, seg)
    full = lambda shape: pl.BlockSpec(shape, lambda s: (0,) * len(shape))
    return pl.pallas_call(
        functools.partial(attend_back_kernel, heads=heads, tile=tile),
        grid=(seqs,),
        in_specs=[
            pl.BlockSpec(memory_space=pltpu.SMEM),
            pl.BlockSpec((blocks, 1, seg, width), lambda s: (0, s, 0, 0)),
            pl.BlockSpec((blocks, 1, seg, heads * HEAD_WIDTH), lambda s: (0, s, 0, 0)),
            pl.BlockSpec((1, heads, length, HEAD_WIDTH), lambda s: (s, 0, 0, 0)),
            full((length, HEAD_WIDTH)),
            full((length, HEAD_WIDTH)),
            full((2, HEAD_WIDTH)),
            pl.BlockSpec((1, 1, length), lambda s: (s, 0, 0)),
        ],
        out_specs=[
            pl.BlockSpec((blocks, 1, seg, width), lambda s: (0, s, 0, 0)),
            pl.BlockSpec((1, 2, HEAD_WIDTH), lambda s: (s, 0, 0)),
        ],
        out_shape=[
            jax.ShapeDtypeStruct((blocks, seqs, seg, width), BF),
            jax.ShapeDtypeStruct((seqs, 2, HEAD_WIDTH), F32),
        ],
        scratch_shapes=[pltpu.VMEM((length, HEAD_WIDTH), F32)] * 3,
        name="attend_back",
    )(places, qkv, grads, lse, cosine, sine, gains, keep)


def rotate(value, ways, move):
    chips = ways // 2
    pairs = [(2 * s + k, 2 * ((s + move) % chips) + k) for s in range(chips) for k in (0, 1)]
    return lax.ppermute(value, "expert", pairs)


def exchange(value, ways):
    return lax.ppermute(value, "expert", [(e, e ^ 1) for e in range(ways)])


def column(block, ways):
    return [block] + [rotate(block, ways, h) for h in range(1, ways // 2)]


def partners(blocks, ways):
    return [exchange(value, ways) for value in blocks]


def pair_up(parts, sources, ways):
    chips = ways // 2
    mine = [take_major(parts, sources[h]) for h in range(chips)]
    other = exchange(jnp.stack([take_major(parts, sources[chips + h]) for h in range(chips)]), ways)
    own = mine[0].astype(F32) + other[0].astype(F32)
    rest = [(mine[h].astype(F32) + other[h].astype(F32)).astype(BF) for h in range(1, chips)]
    return lax.optimization_barrier((own, *rest))


def in_order(blocks, sources):
    whole = jnp.zeros((len(blocks),) + blocks[0].shape, blocks[0].dtype)
    for place, block in enumerate(blocks):
        whole = lax.dynamic_update_index_in_dim(whole, block, sources[place], 0)
    return whole.reshape((-1,) + blocks[0].shape[1:])


def deliver(rest, ways, *earlier):
    return [rotate(after(part, *earlier), ways, -(h + 1)) for h, part in enumerate(rest)]


def total_of(own, arrived):
    for part in arrived:
        own = own + part.astype(F32)
    return own


def after(value, *earlier):
    return lax.optimization_barrier((value,) + earlier)[0]


def take_major(array, index):
    return lax.dynamic_index_in_dim(array, index, 0, keepdims=False)


def body(
    tokens,
    cotangent,
    lengths,
    order,
    routes,
    attn_norm,
    query_weight,
    key_weight,
    value_weight,
    q_norm,
    k_norm,
    output_weight,
    ffn_norm,
    w_router,
    w_gate,
    w_up,
    w_down,
):
    both = ("dp", "expert")
    dps = lax.axis_size("dp")
    ways = lax.axis_size("expert")
    chips = ways // 2
    me = lax.axis_index("expert")
    chip, core = me // 2, me % 2
    seqs, seg, _ = tokens.shape
    length = seg * ways
    blk = SEQ_MB * seg
    own_rows = attn_norm.shape[0]
    experts = w_router.shape[1]
    capacity = blk * TOP // experts
    local = w_gate.shape[0]
    ff = w_gate.shape[2]
    hcols = D // ways
    slots = ways * capacity

    sources = jnp.stack(
        [((chip + chips - h) % chips) * 2 + (core ^ cc) for cc in (0, 1) for h in range(chips)]
    )
    positions = jnp.arange(length, dtype=jnp.int32)
    places = jnp.arange(ways, dtype=jnp.int32)
    inverse = THETA ** (-(2.0 * jnp.arange(HEAD_WIDTH // 2, dtype=F32)) / HEAD_WIDTH)
    angles = positions.astype(F32)[:, None] * inverse[None, :]
    cosine = jnp.concatenate([jnp.cos(angles)] * 2, axis=1)
    sine = jnp.concatenate([-jnp.sin(angles), jnp.sin(angles)], axis=1)
    gains = jnp.stack([q_norm, k_norm]).astype(F32)

    own_gain = attn_norm.astype(F32)[:, None]
    split = lambda weight: (weight.astype(F32) * own_gain).astype(BF).reshape(own_rows, ways, hcols)
    qkv_part = jnp.concatenate(
        [split(query_weight), split(key_weight), split(value_weight)], axis=2
    ).transpose(1, 0, 2)
    qkv_part = lax.all_to_all(qkv_part, "expert", split_axis=0, concat_axis=0, tiled=True)
    w_qkv = lax.all_gather(
        qkv_part.reshape(ways * own_rows, 3 * hcols), "dp", axis=0, tiled=True
    )

    route_cols = routes.astype(BF).reshape(own_rows, -1)
    small = jnp.concatenate([w_router, ffn_norm[:, None], route_cols], axis=1)
    route_end = small.shape[1]
    small = jnp.pad(small, ((0, 0), (0, -route_end % 128)))
    small = lax.all_gather(
        jnp.concatenate([output_weight, small], axis=1), both, axis=0, tiled=True
    )
    w_out, small = small[:, :D], small[:, D:]
    router = small[:, :experts]
    gain_ffn = small[:, experts].astype(F32)[None, :]
    all_routes = lax.dynamic_index_in_dim(
        small[:, experts + 1 : route_end].reshape(dps, ways, own_rows, -1),
        lax.axis_index("dp"),
        0,
        keepdims=False,
    ).reshape(ways, seqs, seg, TOP)
    all_routes = all_routes.transpose(1, 0, 3, 2)

    gate_full = lax.all_gather(w_gate, "dp", axis=1, tiled=True)
    up_full = lax.all_gather(w_up, "dp", axis=1, tiled=True)
    down_full = lax.all_gather(w_down, "dp", axis=1, tiled=True)

    strict = (
        jnp.arange(blk, dtype=jnp.int32)[:, None] < jnp.arange(blk, dtype=jnp.int32)[None, :]
    ).astype(BF)
    slot_ids = jnp.arange(capacity, dtype=jnp.int32)[None, :, None]
    expert_ids = jnp.arange(experts, dtype=jnp.int32)

    def add(total, part):
        return part if total is None else total + part

    def rows_of(array, picks):
        return jnp.concatenate([take_major(array, p) for p in picks], axis=0)

    def attention(s, gathered, *earlier):
        normed = in_order(
            [
                (b * norm_factor(b)).astype(BF)
                for b in (block.astype(F32) for block in gathered)
            ],
            sources,
        )
        qkv = after(dot(normed, w_qkv), *earlier).reshape(ways, SEQ_MB, seg, 3 * hcols)
        mixed, lse = attend(places, qkv, cosine, sine, gains, s.keep)
        vars(s).update(normed=normed, qkv=qkv, lse=lse, mixed_heads=mixed)

    def projection(s, *earlier):
        mixed = lax.all_to_all(
            s.mixed_heads, "expert", split_axis=0, concat_axis=0, tiled=True
        )
        mixed = after(mixed, *earlier).transpose(1, 2, 0, 3).reshape(blk, D)
        hidden = s.rows.astype(F32) + dot(mixed, w_out)
        factor_ffn = norm_factor(hidden)
        routed = (hidden * factor_ffn * gain_ffn).astype(BF)
        vars(s).update(mixed=mixed, hidden=hidden, factor_ffn=factor_ffn, routed=routed)

    def expert_layer(s, routed_all, grad_all, waits):
        routed_blocks = routed_all.reshape(ways, blk, D)
        picked = jnp.stack([take_major(all_routes, p) for p in s.picks], axis=2)
        picked = picked.reshape(ways, TOP, blk).astype(jnp.int32)
        alive = s.live_at.reshape(SEQ_MB, ways, seg).transpose(1, 0, 2).reshape(ways, blk)
        logits = lax.dot_general(
            router, routed_all, (((0,), (1,)), ((), ())), preferred_element_type=F32
        ).reshape(experts, ways, blk)
        chosen = jnp.any(picked[None] == expert_ids[:, None, None, None], axis=2)
        masked = jnp.where(chosen, logits, NEG)
        expo = jnp.exp(masked - jnp.max(masked, axis=0, keepdims=True))
        gates = expo / jnp.sum(expo, axis=0, keepdims=True)
        backs = []
        pin = lambda value, name, j: after(value, *waits.get((name, j), tuple)())
        mixtures = grads_routed = None
        gate_grads = []
        for j in range(local):
            mine = me * local + j
            hits = jnp.any(picked == mine, axis=1) & alive
            rank = dot(hits.astype(BF), strict).astype(jnp.int32)
            select = ((rank[:, None, :] == slot_ids) & hits[:, None, :]).astype(BF)
            gate = take_major(gates, mine)
            slot_gate = jnp.sum(select * gate[:, None, :], axis=2).reshape(slots, 1)
            gather = lambda table: jnp.einsum(
                "bct,btd->bcd", select, table, preferred_element_type=F32
            ).astype(BF).reshape(slots, D)
            combine = lambda made: jnp.einsum(
                "bct,bcd->btd",
                select,
                made.reshape(ways, capacity, D),
                preferred_element_type=F32,
            )
            sent = gather(pin(routed_blocks, "sent", j))
            grad_sent_in = gather(grad_all.reshape(ways, blk, D))
            gate_pre = dot(sent, gate_full[j])
            up_pre = dot(sent, up_full[j])
            sigma = 1.0 / (1.0 + jnp.exp(-gate_pre))
            act = gate_pre * sigma * up_pre
            scaled = (act * slot_gate).astype(BF)
            made = dot(scaled, down_full[j])
            mixtures = add(mixtures, combine(pin(made.astype(BF), "made", j)))
            lifted = dot_nt(grad_sent_in, down_full[j])
            row_dots = jnp.sum(act * lifted, axis=1).reshape(ways, capacity, 1)
            gate_grads.append(jnp.sum(select * row_dots, axis=1))
            grad_act = pin(lifted, "lifted", j) * slot_gate
            grad_up = (grad_act * gate_pre * sigma).astype(BF)
            grad_gate = (grad_act * up_pre * sigma * (1.0 + gate_pre * (1.0 - sigma))).astype(BF)
            grad_in = dot_nt(grad_gate, gate_full[j]) + dot_nt(grad_up, up_full[j])
            grads_routed = add(grads_routed, combine(pin(grad_in.astype(BF), "grad_in", j)))
            backs.append((sent, grad_gate, grad_up, scaled, grad_sent_in))
            s.partial = getattr(s, "partial", grads_routed)
        vars(s).update(
            backs=backs,
            gates=lax.dynamic_index_in_dim(gates, me, 1, keepdims=False),
            gate_grads=jnp.stack(gate_grads, axis=1),
            mixtures=mixtures.astype(BF),
            grads_routed=grads_routed.astype(BF),
        )

    def token_backward(s):
        gate_grad = lax.all_to_all(
            s.gate_grads, "expert", split_axis=0, concat_axis=0, tiled=True
        ).reshape(experts, blk)
        own_gates = s.gates
        grad_logits = own_gates * (
            gate_grad - jnp.sum(own_gates * gate_grad, axis=0, keepdims=True)
        )
        grad_logits = grad_logits.astype(BF)
        grad_routed = s.total_g.astype(F32) + lax.dot_general(
            grad_logits, router, (((0,), (1,)), ((), ())), preferred_element_type=F32
        )
        s.g_router = lax.dot_general(
            s.routed, grad_logits, (((0,), (1,)), ((), ())), preferred_element_type=F32
        )
        hidden, factor_ffn = s.hidden, s.factor_ffn
        s.g_ffn_gain = jnp.sum(grad_routed * hidden * factor_ffn, axis=0, keepdims=True)
        grad_hidden = s.grad_rows.astype(F32) * s.live_col + norm_back(
            grad_routed, hidden, factor_ffn, gain_ffn
        )
        gh = grad_hidden.astype(BF)
        grad_mixed = dot_nt(gh, w_out).astype(BF).reshape(SEQ_MB, seg, ways, hcols)
        grad_mixed = grad_mixed.transpose(2, 0, 1, 3)
        vars(s).update(grad_hidden=grad_hidden, gh=gh, grad_send=grad_mixed)
        s.grad_mixed = lax.all_to_all(
            grad_mixed, "expert", split_axis=0, concat_axis=0, tiled=True
        )

    def attention_backward(s, first, second):
        g_qkv, head_gains = attend_back(
            places, s.qkv, after(s.grad_mixed, *first), s.lse, cosine, sine, gains, s.keep
        )
        s.g_qkv = g_qkv.reshape(ways * blk, 3 * hcols)
        s.g_head_gains = jnp.sum(head_gains, axis=0)
        g_rows = after(s.g_qkv, *second())
        s.parts = dot_nt(g_rows, w_qkv).astype(BF).reshape(ways, blk, D)

    def expert_grad(left, right, *earlier):
        full = jnp.stack(
            [
                sum(
                    dot_tn(after(s.backs[j][left], *earlier), s.backs[j][right])
                    for s in state
                )
                for j in range(local)
            ]
        ).astype(BF)
        return full, lax.psum_scatter(full, "dp", scatter_dimension=1, tiled=True)

    state = []
    for micro in range(MICRO):
        picks = [order[0, micro * SEQ_MB + i] for i in range(SEQ_MB)]
        seq_lens = jnp.stack([lengths[p] for p in picks])
        live_at = positions[None, :] < seq_lens[:, None]
        state.append(
            SimpleNamespace(
                picks=picks,
                live_at=live_at,
                keep=live_at.astype(F32)[:, None, :],
                live_col=lax.dynamic_slice_in_dim(live_at, me * seg, seg, 1)
                .reshape(blk, 1)
                .astype(F32),
                rows=rows_of(tokens, picks),
                grad_rows=rows_of(cotangent, picks),
            )
        )

    one, two = state
    tokens_one = column(one.rows, ways)
    tokens_two = column(two.rows, ways)
    grads_one = column(one.grad_rows, ways)
    attention(
        one,
        [after(block, *tokens_two[1:-1]) for block in tokens_one + partners(tokens_one, ways)],
        grads_one[1],
    )
    tokens_two = [after(block, one.mixed_heads, grads_one[2]) for block in tokens_two]
    projection(one)
    routed_one = column(one.routed, ways)
    attention(two, tokens_two + partners(tokens_two, ways), one.routed, *grads_one[3:])
    routed_one = routed_one + partners(routed_one, ways)
    projection(two, *routed_one[1 : ways // 2])
    grads_one = grads_one + partners(grads_one, ways)
    gather_up = lambda value: lax.all_gather(value, "expert", axis=0, tiled=True)
    scatter_sum = lambda value: lax.psum_scatter(
        value.reshape(ways * blk, D), "expert", scatter_dimension=0, tiled=True
    )
    routed_two = gather_up(two.routed)
    grads_two = gather_up(after(two.grad_rows, two.routed))

    expert_layer(
        one,
        after(in_order(routed_one, sources), two.routed),
        in_order(grads_one, sources),
        {},
    )
    one.total_g = scatter_sum(one.grads_routed)
    total_m = scatter_sum(after(one.mixtures, one.total_g))
    one.total_m = lambda: total_m.astype(F32)
    expert_layer(two, after(routed_two, one.mixtures, one.grads_routed), grads_two, {})
    two.total_g = scatter_sum(after(two.grads_routed, total_m))
    one.total_g = after(one.total_g, two.grads_routed)
    token_backward(one)
    full_gate, grad_w_gate = expert_grad(0, 1, one.grad_send)
    full_up, grad_w_up = expert_grad(0, 2, full_gate)
    full_down, grad_w_down = expert_grad(3, 4, full_up)
    two.total_g = after(two.total_g, full_down)
    token_backward(two)
    two.pair_m = pair_up(two.mixtures, sources, ways)
    two.arrived_m = deliver(two.pair_m[1:], ways)
    attention_backward(one, (two.grad_send, two.arrived_m[0]), lambda: (two.arrived_m[1],))
    one.pair_p = pair_up(one.parts, sources, ways)
    g_out_weight = dot_tn(
        after(jnp.concatenate([s.mixed for s in state], axis=0), one.g_qkv)
        .reshape(-1, dps, 2, D // dps // 2)
        .transpose(0, 2, 1, 3)
        .reshape(-1, D),
        jnp.concatenate([s.gh for s in state], axis=0),
    ).reshape(2, D // 2, D)
    one.arrived_p = deliver(one.pair_p[1:], ways)
    attention_backward(
        two, (g_out_weight, two.arrived_m[-1], one.arrived_p[0]), lambda: (one.arrived_p[1],)
    )
    two.pair_p = pair_up(two.parts, sources, ways)
    two.arrived_p = deliver(two.pair_p[1:], ways, *one.arrived_p)
    g_qkv_weight = sum(
        dot_tn(after(s.normed, one.arrived_p[-1], two.arrived_p[0]), s.g_qkv) for s in state
    )
    two.total_m = lambda: total_of(two.pair_m[0], two.arrived_m)
    g_router = sum(s.g_router for s in state)
    g_ffn_gain = sum(s.g_ffn_gain for s in state)
    g_head_gains = sum(s.g_head_gains for s in state)

    outputs = jnp.zeros(tokens.shape, BF)
    input_grads = jnp.zeros(tokens.shape, F32)
    for s in state:
        result = (
            (s.hidden + s.total_m()) * s.live_col
        ).astype(BF)
        tokens_f32 = s.rows.astype(F32)
        grad_inputs = s.grad_hidden + norm_back(
            total_of(s.pair_p[0], s.arrived_p), tokens_f32, norm_factor(tokens_f32), 1.0
        )
        for i, p in enumerate(s.picks):
            rows = slice(i * seg, (i + 1) * seg)
            outputs = lax.dynamic_update_index_in_dim(outputs, result[rows], p, 0)
            input_grads = lax.dynamic_update_index_in_dim(input_grads, grad_inputs[rows], p, 0)

    split_own = lambda weight: weight.astype(F32).reshape(own_rows, ways, hcols).transpose(1, 0, 2)
    out_part = lax.psum_scatter(
        g_out_weight.astype(BF), "dp", scatter_dimension=1, tiled=True
    ).reshape(ways, own_rows, D)
    out_pair = pair_up(out_part, sources, ways)
    grad_out = total_of(out_pair[0], deliver(out_pair[1:], ways))
    part = lax.psum_scatter(g_qkv_weight.astype(BF), "dp", scatter_dimension=0, tiled=True)
    part = lax.all_to_all(
        after(part, grad_out).reshape(ways, own_rows, 3 * hcols), "expert", split_axis=0, concat_axis=0, tiled=True
    ).astype(F32)
    plain = jnp.sum(
        part[:, :, :hcols] * split_own(query_weight)
        + part[:, :, hcols : 2 * hcols] * split_own(key_weight)
        + part[:, :, 2 * hcols :] * split_own(value_weight),
        axis=(0, 2),
    )
    grad_q, grad_k, grad_v = (
        part[:, :, i * hcols : (i + 1) * hcols].transpose(1, 0, 2).reshape(own_rows, D) * own_gain
        for i in range(3)
    )
    grad_attn_norm = plain
    tiled_gains = jnp.tile(g_head_gains.reshape(2, own_rows, -1), (1, dps * ways, 1))
    small_grads = jnp.concatenate(
        [g_router, g_ffn_gain.T, tiled_gains[0], tiled_gains[1]], axis=1
    )
    small_grads = after(small_grads, *two.arrived_p[1:]).reshape(dps, ways, own_rows, -1)
    small_grads = jnp.sum(
        lax.all_to_all(small_grads, "expert", split_axis=1, concat_axis=1, tiled=True), axis=1
    )
    small_grads = jnp.sum(
        lax.all_to_all(small_grads, "dp", split_axis=0, concat_axis=0, tiled=True), axis=0
    )
    per = HEAD_WIDTH // own_rows
    return (
        outputs,
        input_grads,
        grad_attn_norm,
        grad_q,
        grad_k,
        grad_v,
        small_grads[:, experts + 1 : experts + 1 + per].reshape(HEAD_WIDTH),
        small_grads[:, experts + 1 + per :].reshape(HEAD_WIDTH),
        grad_out,
        small_grads[:, experts],
        small_grads[:, :experts],
        grad_w_gate.astype(F32),
        grad_w_up.astype(F32),
        grad_w_down.astype(F32),
    )


def solution(mesh):
    rows = P(("dp", "expert"), None)
    vector = P(("dp", "expert"))
    seqs = P("dp", "expert", None)
    weights = P("expert", "dp", None)
    return jax.shard_map(
        body,
        mesh=mesh,
        in_specs=(
            seqs,
            seqs,
            P("dp"),
            P("dp", None),
            seqs,
            vector,
            rows,
            rows,
            rows,
            P(),
            P(),
            rows,
            vector,
            rows,
            weights,
            weights,
            weights,
        ),
        out_specs=(
            seqs,
            seqs,
            vector,
            rows,
            rows,
            rows,
            P(),
            P(),
            rows,
            vector,
            rows,
            weights,
            weights,
            weights,
        ),
        check_vma=False,
    )
```
